256 devices in a mesh: seq: 32 (over z, y_lo, core), chan: 8 (over y_hi, x).
Axes of the slice: x: 4, y: 4 (y_hi: 2, y_lo: 2; y = y_hi * 2 + y_lo), z: 8, core: 2. Of those that a mesh axis runs over, the one named last changes fastest.
Arguments:
- projected: bfloat16 [8192, 3, 4096], P('seq', None, 'chan'), may hold values from -6 to 6
- short_weight: float32 [3, 3, 4096], P(None, None, 'chan'), may hold values from -3 to 3
- filters: float32 [512, 8192], P(('chan', 'seq')), may hold values from -1.1 to 1.1
- skip: float32 [4096], P('chan'), may hold values from -3 to 3
- out_weight: bfloat16 [4096, 4096], P('chan', 'seq'), may hold values from -0.09375 to 0.09375
- cotangent: bfloat16 [8192, 4096], P('seq', 'chan'), may hold values from -6 to 6
Outputs:
- mixed: bfloat16 [8192, 4096], P('seq', 'chan')
- projected_grad: bfloat16 [8192, 3, 4096], P('seq', None, 'chan')
- filter_grad: float32 [512, 8192], P(('chan', 'seq'))
The draws below stay inside these ranges and needn't reach their ends.
All inputs are finite; a program needn't handle non-finite values.
Results may differ from the reference program's by a relative error of at most 0.008.
Values may be sent and summed in bfloat16 or wider, within the bound.
No kernel may reach another device: no remote copies, remote signals or barrier semaphores. Data moves between devices by JAX's collectives and lax.ppermute only.
A program may use at most 64 MiB of HBM per device.

```python
import math
import jax
import jax.numpy as jnp
from jax import lax

D = 4096
GROUP = 8
SHORT = 3
TOKENS = 8192
G = 512


def draw_filters(key, part):
    keys = jax.random.split(key, 4)
    slow_share = 0.5
    slow = jax.random.uniform(keys[0], (G, 1), jnp.float32) < slow_share
    slow_rate = jnp.exp(jax.random.uniform(keys[1], (G, 1), jnp.float32, math.log(0.2 / TOKENS), math.log(2.0 / TOKENS)))
    fast_rate = jnp.exp(jax.random.uniform(keys[2], (G, 1), jnp.float32, math.log(1.0 / 50.0), math.log(1.0 / 30.0)))
    rate = jnp.where(slow, slow_rate, fast_rate)
    position = jnp.arange(TOKENS, dtype=jnp.float32)[None, :]
    noise = jax.random.truncated_normal(keys[3], -4.0, 4.0, (G, TOKENS), jnp.float32)
    scale = jnp.sqrt((1.0 - jnp.exp(-2.0 * rate)) / (1.0 - jnp.exp(-2.0 * rate * TOKENS)))
    return (noise * jnp.exp(-rate * position) * scale).astype(jnp.float32)


def steps_of(stream_key, extent, shards, low, largest):
    def one(dim, blocks):
        draws = jax.random.uniform(jax.random.fold_in(jax.random.fold_in(stream_key, 6), dim), (blocks,), jnp.float32, low / len(shards), largest / len(shards))
        return jnp.repeat(jnp.exp(draws), extent[dim] // blocks).reshape((-1,) + (1,) * (len(extent) - dim - 1))

    gain = one(*shards[0])
    for cut in shards[1:]:
        gain = gain * one(*cut)
    return gain


def gaussian(stream_key, extent, deviation, most, cuts=(), kind=jnp.bfloat16):
    entries = jax.random.normal(stream_key, extent, jnp.float32) * deviation
    if len(cuts) > 0:
        entries = steps_of(stream_key, extent, cuts, -0.22, 0.18) * entries
    return jnp.clip(entries, min=-most, max=most).astype(kind)


def setup_inputs(seed: int = 0) -> dict:
    seeds = jax.random.split(jax.random.key(seed), 7)
    return {
        "projected": gaussian(seeds[0], (TOKENS, 3, D), 1.0, 6.0, ((0, 32), (2, 8))),
        "short_weight": gaussian(seeds[1], (3, SHORT, D), 0.6, 3.0, ((2, 8),), jnp.float32),
        "filters": draw_filters(jax.random.fold_in(seeds[6], 71), 0),
        "skip": gaussian(seeds[3], (D,), 1.0, 3.0, ((0, 8),), jnp.float32),
        "out_weight": gaussian(seeds[4], (D, D), D ** -0.5, 0.09375, ((0, 8), (1, 32))),
        "cotangent": gaussian(seeds[5], (TOKENS, D), 1.0, 6.0, ((0, 32), (1, 8))),
    }


def grouped(spectrum):
    return spectrum.reshape(G, GROUP, spectrum.shape[-1])

def reference(projected, short_weight, filters, skip, out_weight, cotangent):
    length = TOKENS
    rim = SHORT - 1
    values = projected.astype(jnp.float32)
    padded = jnp.pad(values, ((rim, 0), (0, 0), (0, 0)))
    short = sum((short_weight[:, j, :] * padded[j:j + length] for j in range(SHORT)))
    query_side = short[:, 0]
    key_side = short[:, 1]
    value_side = short[:, 2]
    carried = (key_side * value_side).astype(jnp.bfloat16)
    spec_kv = jnp.fft.rfft(carried.astype(jnp.float32).T, n=2 * length, axis=-1)
    spec_h = jnp.fft.rfft(filters, n=2 * length, axis=-1)
    conv_spec = (grouped(spec_kv) * spec_h[:, None, :]).reshape(D, -1)
    conv = jnp.fft.irfft(conv_spec, n=2 * length, axis=-1)[:, :length].T.astype(jnp.bfloat16)
    mixed_in = conv.astype(jnp.float32) + skip * carried.astype(jnp.float32)
    gated = (query_side * mixed_in).astype(jnp.bfloat16)
    mixed = jnp.dot(gated, out_weight, preferred_element_type=jnp.float32).astype(jnp.bfloat16)
    gated_grad = jnp.dot(cotangent, out_weight.T, preferred_element_type=jnp.float32)
    query_grad = gated_grad * mixed_in
    mixed_grad = (gated_grad * query_side).astype(jnp.bfloat16)
    spec_dy = jnp.fft.rfft(mixed_grad.astype(jnp.float32).T, n=2 * length, axis=-1)
    back_spec = (grouped(spec_dy) * jnp.conj(spec_h)[:, None, :]).reshape(D, -1)
    back = jnp.fft.irfft(back_spec, n=2 * length, axis=-1)[:, :length].T.astype(jnp.bfloat16)
    cross = lax.optimization_barrier(jnp.sum(grouped(spec_dy) * jnp.conj(grouped(spec_kv)), axis=1))
    filter_grad = jnp.fft.irfft(cross, n=2 * length, axis=-1)[:, :length] * (1.0 / math.sqrt(GROUP * TOKENS))
    carried_grad = back.astype(jnp.float32) + skip * mixed_grad.astype(jnp.float32)
    short_grad = jnp.stack([query_grad, carried_grad * value_side, carried_grad * key_side], axis=1)
    padded_grad = jnp.pad(short_grad, ((0, rim), (0, 0), (0, 0)))
    projected_grad = sum((short_weight[:, j, :] * padded_grad[rim - j:rim - j + length] for j in range(SHORT)))
    return (mixed, projected_grad.astype(jnp.bfloat16), filter_grad.astype(jnp.float32))
```

```python
import functools
import math

import jax
import jax.numpy as jnp
from jax import lax
from jax.experimental import pallas as pl
from jax.experimental.pallas import tpu as pltpu
from jax.sharding import Mesh, PartitionSpec as P

GROUP = 8
SHORT = 3
BLOCK = 256
HALF = 128

SEQ = ("z", "yl", "core")
CHAN = ("yh", "x")
F32 = jnp.float32
BF16 = jnp.bfloat16


def from_behind(shard, by):
    count = lax.axis_size(SEQ)
    pairs = [(i, i + by) for i in range(count) if 0 <= i + by < count]
    return lax.ppermute(shard, SEQ, pairs)


def swap(shard, axis):
    return lax.ppermute(shard, axis, [(0, 1), (1, 0)])


def gathered(shard, axes, count):
    copies = jnp.broadcast_to(shard[None], (count,) + shard.shape)
    return lax.all_to_all(copies, axes, split_axis=0, concat_axis=0, tiled=True)


def skew_masks():
    rows = lax.broadcasted_iota(jnp.int32, (HALF, HALF), 0)
    lanes = lax.broadcasted_iota(jnp.int32, (HALF, HALF), 1)
    return rows, lanes


def build_toeplitz(h_ref, g, tile_ref):
    count = h_ref.shape[1]
    rows, lanes = skew_masks()
    tile_ref[0] = jnp.zeros((HALF, HALF), BF16)

    def step(j, before):
        row = h_ref[g, pl.ds(j, 1), :]
        turned = pltpu.roll(jnp.broadcast_to(row, (HALF, HALF)), 0, 1, stride=1, stride_axis=0)
        tile_ref[j + 1] = jnp.where(lanes >= rows, turned, before).astype(BF16)
        return turned

    lax.fori_loop(0, count, step, jnp.zeros((HALF, HALF), F32))


def toeplitz_block(tile_ref, d):
    same = tile_ref[2 * d + 1]
    upper = jnp.concatenate([same, tile_ref[2 * d + 2]], axis=1)
    lower = jnp.concatenate([tile_ref[2 * d], same], axis=1)
    return jnp.concatenate([upper, lower], axis=0)


def group_rows(ref, g):
    part = ref[...].astype(F32)[:, g * GROUP : (g + 1) * GROUP, :]
    return part.reshape(part.shape[0] * GROUP, BLOCK)


def segments(blocks):
    half = blocks // 2
    return ((0, half, blocks * GROUP), (half, blocks, half * GROUP))


def conv_kernel(x_ref, h_ref, y_ref, tile_ref, acc_ref):
    blocks, chans, _ = x_ref.shape
    parts = []
    for g in range(chans // GROUP):
        build_toeplitz(h_ref, g, tile_ref)
        signal = group_rows(x_ref, g).astype(BF16)
        acc_ref[...] = jnp.zeros_like(acc_ref)
        for low, high, rows in segments(blocks):
            lhs = signal[:rows]

            def step(d, carry, lhs=lhs, rows=rows):
                at = pl.ds(pl.multiple_of(d * GROUP, GROUP), rows)
                acc_ref[at, :] += jnp.dot(
                    lhs, toeplitz_block(tile_ref, d), preferred_element_type=F32
                )
                return carry

            lax.fori_loop(low, high, step, 0)
        parts.append(acc_ref[: blocks * GROUP, :].reshape(blocks, GROUP, BLOCK))
    y_ref[...] = jnp.concatenate(parts, axis=1).astype(BF16)


def back_kernel(m_ref, x_ref, h_ref, y_ref, f_ref, tile_ref, grad_ref, acc_ref, low_ref, high_ref, *, scale):
    blocks, chans, _ = x_ref.shape
    total = blocks * GROUP
    rows_i, lanes_i = skew_masks()
    wrapped = lanes_i <= rows_i
    flip = (
        lax.broadcasted_iota(jnp.int32, (BLOCK, BLOCK), 0)
        + lax.broadcasted_iota(jnp.int32, (BLOCK, BLOCK), 1)
        == BLOCK - 1
    )
    flip = jnp.where(flip, 1.0, 0.0).astype(BF16)
    parts = []

    def fold(v):
        return v.reshape(HALF // 8, 8, HALF).sum(axis=0)

    for g in range(chans // GROUP):
        build_toeplitz(h_ref, g, tile_ref)
        grad_ref[:total, :] = group_rows(m_ref, g)
        grad_ref[total:, :] = jnp.zeros((grad_ref.shape[0] - total, BLOCK), F32)
        signal = group_rows(x_ref, g).astype(BF16)
        flipped = lax.dot_general(
            flip, signal, (((1,), (1,)), ((), ())), preferred_element_type=F32
        ).astype(BF16)
        acc_ref[...] = jnp.zeros_like(acc_ref)
        high_ref[blocks] = jnp.zeros((8, BLOCK), F32)
        for low, high, rows in segments(blocks):
            lhs = flipped[:, :rows]

            def step(d, carry, lhs=lhs, rows=rows):
                at = pl.ds(pl.multiple_of(d * GROUP, GROUP), rows)
                grad = grad_ref[at, :].astype(BF16)
                acc_ref[:rows, :] += lax.dot_general(
                    grad,
                    toeplitz_block(tile_ref, d),
                    (((1,), (1,)), ((), ())),
                    preferred_element_type=F32,
                )
                cross = jnp.dot(lhs, grad, preferred_element_type=F32)
                turn = [
                    pltpu.roll(
                        cross[r * HALF : (r + 1) * HALF, l * HALF : (l + 1) * HALF],
                        1,
                        1,
                        stride=1,
                        stride_axis=0,
                    )
                    for r in range(2)
                    for l in range(2)
                ]
                s00, s01, s10, s11 = turn
                zero = jnp.zeros((HALF, HALF), F32)
                low0 = jnp.where(wrapped, s01 + s10, s11)
                high0 = jnp.where(wrapped, zero, s00)
                low1 = jnp.where(wrapped, s11, zero)
                high1 = jnp.where(wrapped, s00, s01 + s10)
                low_ref[d] = jnp.concatenate([fold(low0), fold(low1)], axis=1)
                high_ref[d] = jnp.concatenate([fold(high0), fold(high1)], axis=1)
                return carry

            lax.fori_loop(low, high, step, 0)
        parts.append(acc_ref[...].reshape(blocks, GROUP, BLOCK))
        f_ref[g] = (low_ref[...] + high_ref[pl.ds(1, blocks)]).sum(axis=1) * scale
    y_ref[...] = jnp.concatenate(parts, axis=1).astype(BF16)


def conv_forward(x, h):
    blocks = x.shape[0]
    return pl.pallas_call(
        conv_kernel,
        name="conv_forward",
        out_shape=jax.ShapeDtypeStruct(x.shape, BF16),
        scratch_shapes=[
            pltpu.VMEM((h.shape[1] + 1, HALF, HALF), BF16),
            pltpu.VMEM((blocks * GROUP + blocks // 2 * GROUP, BLOCK), F32),
        ],
        cost_estimate=pl.CostEstimate(flops=2000000000, bytes_accessed=600000, transcendentals=0),
    )(x, h)


def conv_backward(m, x, h):
    blocks, chans, _ = x.shape
    scale = 1.0 / math.sqrt(GROUP * blocks * BLOCK)
    return pl.pallas_call(
        functools.partial(back_kernel, scale=scale),
        name="conv_backward",
        out_shape=(
            jax.ShapeDtypeStruct(x.shape, BF16),
            jax.ShapeDtypeStruct((chans // GROUP, blocks, BLOCK), F32),
        ),
        scratch_shapes=[
            pltpu.VMEM((h.shape[1] + 1, HALF, HALF), BF16),
            pltpu.VMEM((blocks * GROUP + blocks // 2 * GROUP, BLOCK), F32),
            pltpu.VMEM((blocks * GROUP, BLOCK), F32),
            pltpu.VMEM((blocks, 8, BLOCK), F32),
            pltpu.VMEM((blocks + 1, 8, BLOCK), F32),
        ],
        cost_estimate=pl.CostEstimate(flops=4000000000, bytes_accessed=1000000, transcendentals=0),
    )(m, x, h)


def quarter_columns(q_ref, k, width):
    return pl.ds(pl.multiple_of(q_ref[k] * width, width), width)


def grad_mm_kernel(q_ref, cot_ref, *refs):
    *w_refs, out_ref = refs
    total = None
    for k, w_ref in enumerate(w_refs):
        width = w_ref.shape[2]
        part = lax.dot_general(
            cot_ref[0, :, quarter_columns(q_ref, k, width)],
            w_ref[0],
            (((1,), (1,)), ((), ())),
            preferred_element_type=F32,
        )
        total = part if total is None else total + part

    @pl.when(pl.program_id(0) == 0)
    def _():
        out_ref[...] = total

    @pl.when(pl.program_id(0) != 0)
    def _():
        out_ref[...] += total


def grad_matmul(quarters, cot, ws):
    count, tok, cols = cot.shape
    _, rows, width = ws[0].shape
    return pl.pallas_call(
        grad_mm_kernel,
        name="grad_matmul",
        out_shape=jax.ShapeDtypeStruct((tok, rows), F32),
        grid_spec=pltpu.PrefetchScalarGridSpec(
            num_scalar_prefetch=1,
            grid=(count,),
            in_specs=[pl.BlockSpec((1, tok, cols), lambda i, q: (i, 0, 0))]
            + [pl.BlockSpec((1, rows, width), lambda i, q: (i, 0, 0))] * len(ws),
            out_specs=pl.BlockSpec((tok, rows), lambda i, q: (0, 0)),
        ),
        cost_estimate=pl.CostEstimate(flops=1100000000, bytes_accessed=6500000, transcendentals=0),
    )(quarters, cot, *ws)


def mix_mm_kernel(q_ref, gated_ref, *refs):
    *w_refs, out_ref = refs
    gated = gated_ref[...]
    for k, w_ref in enumerate(w_refs):
        width = w_ref.shape[2]
        out_ref[0, :, quarter_columns(q_ref, k, width)] = jnp.dot(
            gated, w_ref[0], preferred_element_type=F32
        ).astype(BF16)


def mix_matmul(quarters, gated, ws):
    tok, rows = gated.shape
    count, _, width = ws[0].shape
    cols = width * len(ws)
    return pl.pallas_call(
        mix_mm_kernel,
        name="mix_matmul",
        out_shape=jax.ShapeDtypeStruct((count, tok, cols), BF16),
        grid_spec=pltpu.PrefetchScalarGridSpec(
            num_scalar_prefetch=1,
            grid=(count,),
            in_specs=[pl.BlockSpec((tok, rows), lambda i, q: (0, 0))]
            + [pl.BlockSpec((1, rows, width), lambda i, q: (i, 0, 0))] * len(ws),
            out_specs=pl.BlockSpec((1, tok, cols), lambda i, q: (i, 0, 0)),
        ),
        cost_estimate=pl.CostEstimate(flops=1100000000, bytes_accessed=6500000, transcendentals=0),
    )(quarters, gated, *ws)


def channel_major(block):
    count = lax.axis_size(SEQ)
    sent = block.T.reshape(count, block.shape[1] // count, block.shape[0])
    return lax.all_to_all(sent, SEQ, split_axis=0, concat_axis=0, tiled=True)


def token_major(block):
    got = lax.all_to_all(block, SEQ, split_axis=0, concat_axis=0, tiled=True)
    return got.reshape(got.shape[0] * got.shape[1], got.shape[2]).T


def on_device(projected, short_weight, filters, skip, out_weight, cotangent):
    tok_rows = projected.shape[0]
    groups_dev, seq_length = filters.shape
    rim = SHORT - 1
    h = filters.reshape(groups_dev, seq_length // HALF, HALF)

    before = from_behind(projected[tok_rows - rim :], 1)
    cot = gathered(cotangent, CHAN, lax.axis_size(CHAN))
    w_own = gathered(out_weight, "z", lax.axis_size("z"))

    extended = jnp.concatenate([before, projected], axis=0).astype(F32)
    short = short_weight[:, 0, :] * extended[0:tok_rows]
    for j in range(1, SHORT):
        short = short + short_weight[:, j, :] * extended[j : j + tok_rows]
    query_side = short[:, 0]
    key_side = short[:, 1]
    value_side = short[:, 2]
    carried = (key_side * value_side).astype(BF16)
    carried_seq = channel_major(carried)
    conv_seq = conv_forward(carried_seq, h)
    conv = token_major(conv_seq)

    w_side = swap(w_own, "yl")
    w_own_other = swap(w_own, "core")
    w_side_other = swap(w_side, "core")
    ws = (w_own, w_own_other, w_side, w_side_other)
    yl, core = lax.axis_index("yl"), lax.axis_index("core")
    quarters = jnp.stack(
        [yl * 2 + core, yl * 2 + 1 - core, (1 - yl) * 2 + core, (1 - yl) * 2 + 1 - core]
    ).astype(jnp.int32)

    gated_grad = grad_matmul(quarters, cot, ws)
    mixed_grad = (gated_grad * query_side).astype(BF16)
    grad_seq = channel_major(mixed_grad)

    mixed_in = conv.astype(F32) + skip * carried.astype(F32)
    gated = (query_side * mixed_in).astype(BF16)
    partial = mix_matmul(quarters, gated, ws)
    shares = lax.all_to_all(partial, CHAN, split_axis=0, concat_axis=0, tiled=True)
    mixed = jnp.sum(shares.astype(F32), axis=0).astype(BF16)

    back_seq, filter_grad = conv_backward(grad_seq, carried_seq, h)
    back = token_major(back_seq)
    query_grad = gated_grad * mixed_in
    carried_grad = back.astype(F32) + skip * mixed_grad.astype(F32)
    short_grad = jnp.stack([query_grad, carried_grad * value_side, carried_grad * key_side], axis=1)
    after = from_behind(short_grad[:rim], -1)
    extended_grad = jnp.concatenate([short_grad, after], axis=0)
    projected_grad = short_weight[:, 0, :] * extended_grad[rim : rim + tok_rows]
    for j in range(1, SHORT):
        projected_grad = (
            projected_grad + short_weight[:, j, :] * extended_grad[rim - j : rim - j + tok_rows]
        )
    return (mixed, projected_grad.astype(BF16), filter_grad.reshape(groups_dev, seq_length))


def solution(mesh):
    fine = Mesh(mesh.devices.reshape(8, 2, 2, 2, 4), ("z", "yl", "core", "yh", "x"))
    placed = (
        P(SEQ, None, CHAN),
        P(None, None, CHAN),
        P(CHAN + SEQ, None),
        P(CHAN),
        P(CHAN, SEQ),
        P(SEQ, CHAN),
    )
    return jax.shard_map(
        on_device,
        mesh=fine,
        in_specs=placed,
        out_specs=(P(SEQ, CHAN), P(SEQ, None, CHAN), P(CHAN + SEQ, None)),
        check_vma=False,
    )
```

```python
import functools
import math

import jax
import jax.numpy as jnp
from jax import lax
from jax.experimental import pallas as pl
from jax.experimental.pallas import tpu as pltpu
from jax.sharding import Mesh, PartitionSpec as P


GROUP = 8
SHORT = 3
BLOCK = 256
HALF = 128
LAGS = 4
BUILD_UNROLL = 16

SEQ = ("z", "yl", "core")
CHAN = ("yh", "x")
F32 = jnp.float32
BF16 = jnp.bfloat16


def from_behind(shard, by):
    count = lax.axis_size(SEQ)
    pairs = [(i, i + by) for i in range(count) if 0 <= i + by < count]
    return lax.ppermute(shard, SEQ, pairs)


def swap(shard, axis):
    return lax.ppermute(shard, axis, [(0, 1), (1, 0)])


def gathered(shard, axes, count):
    copies = jnp.broadcast_to(shard[None], (count,) + shard.shape)
    return lax.all_to_all(copies, axes, split_axis=0, concat_axis=0, tiled=True)


def skew_masks():
    rows = lax.broadcasted_iota(jnp.int32, (HALF, HALF), 0)
    lanes = lax.broadcasted_iota(jnp.int32, (HALF, HALF), 1)
    return rows, lanes


def toeplitz_kernel(h_ref, tile_ref):
    groups, count, _ = h_ref.shape
    rows, lanes = skew_masks()
    inside = lanes >= rows
    for g in range(groups):
        tile_ref[g, 0] = jnp.zeros((HALF, HALF), BF16)

        def step(j, before, g=g):
            row = h_ref[g, pl.ds(j, 1), :]
            turned = pltpu.roll(jnp.broadcast_to(row, (HALF, HALF)), 0, 1, stride=1, stride_axis=0)
            tile_ref[g, j + 1] = jnp.where(inside, turned, before).astype(BF16)
            return turned

        lax.fori_loop(0, count, step, jnp.zeros((HALF, HALF), F32), unroll=BUILD_UNROLL)


def toeplitz_tiles(h):
    groups, count, _ = h.shape
    return pl.pallas_call(
        toeplitz_kernel,
        name="toeplitz_tiles",
        out_shape=jax.ShapeDtypeStruct((groups, count + 1, HALF, HALF), BF16),
        cost_estimate=pl.CostEstimate(flops=4000000, bytes_accessed=4500000, transcendentals=0),
    )(h)


def toeplitz_block(tile_ref, g, d):
    same = tile_ref[g, 2 * d + 1]
    upper = jnp.concatenate([same, tile_ref[g, 2 * d + 2]], axis=1)
    lower = jnp.concatenate([tile_ref[g, 2 * d], same], axis=1)
    return jnp.concatenate([upper, lower], axis=0)


def group_rows(ref, g):
    part = ref[...].astype(F32)[:, g * GROUP : (g + 1) * GROUP, :]
    return part.reshape(part.shape[0] * GROUP, BLOCK)


def conv_kernel(x_ref, tile_ref, y_ref, wide_ref, acc_ref):
    blocks, chans, _ = x_ref.shape
    total = blocks * GROUP
    parts = []
    for g in range(chans // GROUP):
        signal = group_rows(x_ref, g)
        for k in range(LAGS):
            late = signal
            if k > 0:
                late = jnp.concatenate(
                    [jnp.zeros((k * GROUP, BLOCK), F32), signal[: total - k * GROUP]], axis=0
                )
            wide_ref[:, k * BLOCK : (k + 1) * BLOCK] = late.astype(BF16)
        for d in range(0, blocks, LAGS):
            rows = total - d * GROUP
            weights = jnp.concatenate(
                [toeplitz_block(tile_ref, g, d + k) for k in range(LAGS)], axis=0
            )
            part = jnp.dot(wide_ref[:rows, :], weights, preferred_element_type=F32)
            if d == 0:
                acc_ref[...] = part
            else:
                acc_ref[d * GROUP :, :] += part
        parts.append(acc_ref[...].reshape(blocks, GROUP, BLOCK))
    y_ref[...] = jnp.concatenate(parts, axis=1).astype(BF16)


def back_kernel(m_ref, x_ref, tile_ref, y_ref, f_ref, wide_ref, acc_ref, low_ref, high_ref, *, scale):
    blocks, chans, _ = x_ref.shape
    total = blocks * GROUP
    rows_i, lanes_i = skew_masks()
    wrapped = lanes_i <= rows_i
    flip = (
        lax.broadcasted_iota(jnp.int32, (BLOCK, BLOCK), 0)
        + lax.broadcasted_iota(jnp.int32, (BLOCK, BLOCK), 1)
        == BLOCK - 1
    )
    flip = jnp.where(flip, 1.0, 0.0).astype(BF16)
    zero = jnp.zeros((HALF, HALF), F32)
    parts = []

    def fold(v):
        return v.reshape(HALF // 8, 8, HALF).sum(axis=0)

    def turned(cross, r, l):
        return pltpu.roll(
            cross[r * HALF : (r + 1) * HALF, l * HALF : (l + 1) * HALF], 1, 1, stride=1, stride_axis=0
        )

    for g in range(chans // GROUP):
        grad = group_rows(m_ref, g)
        wide_ref[total:, :] = jnp.zeros((wide_ref.shape[0] - total, LAGS * BLOCK), BF16)
        for k in range(LAGS):
            early = grad
            if k > 0:
                early = jnp.concatenate(
                    [grad[k * GROUP :], jnp.zeros((k * GROUP, BLOCK), F32)], axis=0
                )
            wide_ref[:total, k * BLOCK : (k + 1) * BLOCK] = early.astype(BF16)
        signal = group_rows(x_ref, g).astype(BF16)
        flipped = lax.dot_general(
            flip, signal, (((1,), (1,)), ((), ())), preferred_element_type=F32
        ).astype(BF16)
        high_ref[blocks] = jnp.zeros((8, BLOCK), F32)
        for d in range(0, blocks, LAGS):
            rows = total - d * GROUP
            weights = jnp.concatenate(
                [toeplitz_block(tile_ref, g, d + k) for k in range(LAGS)], axis=1
            )
            part = lax.dot_general(
                wide_ref[d * GROUP : total, :],
                weights,
                (((1,), (1,)), ((), ())),
                preferred_element_type=F32,
            )
            if d == 0:
                acc_ref[...] = part
            else:
                acc_ref[:rows, :] += part
            depth = total if 2 * d < blocks else total // 2
            cross_all = jnp.dot(
                flipped[:, :depth],
                wide_ref[d * GROUP : d * GROUP + depth, :],
                preferred_element_type=F32,
            )
            for k in range(LAGS):
                cross = cross_all[:, k * BLOCK : (k + 1) * BLOCK]
                s00, s01, s10, s11 = (turned(cross, r, l) for r in range(2) for l in range(2))
                low0 = jnp.where(wrapped, s01 + s10, s11)
                high0 = jnp.where(wrapped, zero, s00)
                low1 = jnp.where(wrapped, s11, zero)
                high1 = jnp.where(wrapped, s00, s01 + s10)
                low_ref[d + k] = jnp.concatenate([fold(low0), fold(low1)], axis=1)
                high_ref[d + k] = jnp.concatenate([fold(high0), fold(high1)], axis=1)
        parts.append(acc_ref[...].reshape(blocks, GROUP, BLOCK))
        f_ref[g] = (low_ref[...] + high_ref[pl.ds(1, blocks)]).sum(axis=1) * scale
    y_ref[...] = jnp.concatenate(parts, axis=1).astype(BF16)


def conv_forward(x, tiles):
    blocks = x.shape[0]
    total = blocks * GROUP
    return pl.pallas_call(
        conv_kernel,
        name="conv_forward",
        out_shape=jax.ShapeDtypeStruct(x.shape, BF16),
        scratch_shapes=[
            pltpu.VMEM((total, LAGS * BLOCK), BF16),
            pltpu.VMEM((total, BLOCK), F32),
        ],
        cost_estimate=pl.CostEstimate(flops=6000000000, bytes_accessed=600000, transcendentals=0),
    )(x, tiles)


def conv_backward(m, x, tiles):
    blocks, chans, _ = x.shape
    total = blocks * GROUP
    scale = 1.0 / math.sqrt(GROUP * blocks * BLOCK)
    return pl.pallas_call(
        functools.partial(back_kernel, scale=scale),
        name="conv_backward",
        out_shape=(
            jax.ShapeDtypeStruct(x.shape, BF16),
            jax.ShapeDtypeStruct((chans // GROUP, blocks, BLOCK), F32),
        ),
        scratch_shapes=[
            pltpu.VMEM((total + total // 2, LAGS * BLOCK), BF16),
            pltpu.VMEM((total, BLOCK), F32),
            pltpu.VMEM((blocks, 8, BLOCK), F32),
            pltpu.VMEM((blocks + 1, 8, BLOCK), F32),
        ],
        cost_estimate=pl.CostEstimate(flops=10000000000, bytes_accessed=1000000, transcendentals=0),
    )(m, x, tiles)


def whole_columns(core, own_ref, other_ref):
    first = core == 0
    own, other = own_ref[0], other_ref[0]
    return jnp.concatenate(
        [jnp.where(first, own, other), jnp.where(first, other, own)], axis=1
    )


def side_columns(side, width):
    return pl.ds(pl.multiple_of(side * width, width), width)


def grad_mm_kernel(
    at_ref, query_ref, cot0, cot1, cot2, cot3, own, own_c, side, side_c, out_ref, mixed_ref, sent_ref
):
    step = pl.program_id(0)
    yl, core = at_ref[0], at_ref[1]
    near = whole_columns(core, own, own_c)
    far = whole_columns(core, side, side_c)
    width = near.shape[1]

    def product(cot_ref, weights, at):
        return lax.dot_general(
            cot_ref[0, :, side_columns(at, width)],
            weights,
            (((1,), (1,)), ((), ())),
            preferred_element_type=F32,
        )

    @pl.when(step == 0)
    def _():
        out_ref[...] = jnp.zeros_like(out_ref)

    for k, cot_ref in enumerate((cot0, cot1, cot2, cot3)):

        @pl.when(step // 2 == k)
        def _(cot_ref=cot_ref):
            out_ref[...] += product(cot_ref, near, yl) + product(cot_ref, far, 1 - yl)

    @pl.when(step == pl.num_programs(0) - 1)
    def _():
        mixed = (out_ref[...] * query_ref[...]).astype(BF16)
        mixed_ref[...] = mixed
        sent_ref[...] = mixed.astype(F32).T.astype(BF16)


def own_turn(k):
    def index(i, q):
        return jnp.clip(i - 2 * k, 0, 1), 0, 0

    return index


def grad_matmul(at, query, cots, ws):
    _, tok, cols = cots[0].shape
    count, rows, width = ws[0].shape
    return pl.pallas_call(
        grad_mm_kernel,
        name="grad_matmul",
        out_shape=(
            jax.ShapeDtypeStruct((tok, rows), F32),
            jax.ShapeDtypeStruct((tok, rows), BF16),
            jax.ShapeDtypeStruct((rows, tok), BF16),
        ),
        grid_spec=pltpu.PrefetchScalarGridSpec(
            num_scalar_prefetch=1,
            grid=(count,),
            in_specs=[pl.BlockSpec((tok, rows), lambda i, q: (0, 0))]
            + [pl.BlockSpec((1, tok, cols), own_turn(k)) for k in range(len(cots))]
            + [pl.BlockSpec((1, rows, width), lambda i, q: (q[2 + i], 0, 0))] * len(ws),
            out_specs=(
                pl.BlockSpec((tok, rows), lambda i, q: (0, 0)),
                pl.BlockSpec((tok, rows), lambda i, q: (0, 0)),
                pl.BlockSpec((rows, tok), lambda i, q: (0, 0)),
            ),
        ),
        cost_estimate=pl.CostEstimate(flops=4000000000, bytes_accessed=6500000, transcendentals=0),
    )(at, query, *cots, *ws)


def mix_mm_kernel(
    at_ref, conv_ref, query_ref, carried_ref, skip_ref, own, own_c, side, side_c,
    out0, out1, out2, out3, mixed_ref, gated_ref,
):
    step = pl.program_id(0)
    yl, core = at_ref[0], at_ref[1]

    @pl.when(step == 0)
    def _():
        conv = conv_ref[...].astype(F32).T
        mixed_in = conv + skip_ref[...] * carried_ref[...].astype(F32)
        mixed_ref[...] = mixed_in
        gated_ref[...] = (query_ref[...] * mixed_in).astype(BF16)

    gated = gated_ref[...]
    near = whole_columns(core, own, own_c)
    far = whole_columns(core, side, side_c)
    width = near.shape[1]
    near = jnp.dot(gated, near, preferred_element_type=F32).astype(BF16)
    far = jnp.dot(gated, far, preferred_element_type=F32).astype(BF16)
    for k, out_ref in enumerate((out0, out1, out2, out3)):

        @pl.when(step // 2 == k)
        def _(out_ref=out_ref):
            out_ref[0, :, side_columns(yl, width)] = near
            out_ref[0, :, side_columns(1 - yl, width)] = far


def mix_matmul(at, conv, query, carried, skip, ws):
    tok, rows = query.shape
    count, _, width = ws[0].shape
    cols = len(ws) * width
    whole = pl.BlockSpec((tok, rows), lambda i, q: (0, 0))
    *parts, mixed_in = pl.pallas_call(
        mix_mm_kernel,
        name="mix_matmul",
        out_shape=(jax.ShapeDtypeStruct((2, tok, cols), BF16),) * (count // 2)
        + (jax.ShapeDtypeStruct((tok, rows), F32),),
        grid_spec=pltpu.PrefetchScalarGridSpec(
            num_scalar_prefetch=1,
            grid=(count,),
            in_specs=[
                pl.BlockSpec((rows, tok), lambda i, q: (0, 0)),
                whole,
                whole,
                pl.BlockSpec((1, rows), lambda i, q: (0, 0)),
            ]
            + [pl.BlockSpec((1, rows, width), lambda i, q: (q[2 + i], 0, 0))] * len(ws),
            out_specs=[pl.BlockSpec((1, tok, cols), own_turn(k)) for k in range(count // 2)]
            + [whole],
            scratch_shapes=[pltpu.VMEM((tok, rows), BF16)],
        ),
        cost_estimate=pl.CostEstimate(flops=4000000000, bytes_accessed=6500000, transcendentals=0),
    )(at, conv, query, carried, skip[None, :], *ws)
    return parts, mixed_in


def shift_x(shard, by):
    count = lax.axis_size("x")
    return lax.ppermute(shard, "x", [(i, (i + by) % count) for i in range(count)])


def pre_kernel(proj_ref, before_ref, taps_ref, query_ref, key_ref, value_ref, carried_ref, sent_ref):
    row = lax.broadcasted_iota(jnp.int32, proj_ref.shape[1:], 0)
    sides = []
    for i in range(3):
        now = proj_ref[i].astype(F32)
        before = before_ref[i].astype(F32)
        total = taps_ref[i, SHORT - 1 : SHORT, :] * now
        for j in range(1, SHORT):
            late = pltpu.roll(now, j, 0)
            for r in range(j):
                late = jnp.where(row == r, before[SHORT - 1 - j + r][None, :], late)
            total = total + taps_ref[i, SHORT - 1 - j : SHORT - j, :] * late
        sides.append(total)
    query_ref[...], key_ref[...], value_ref[...] = sides
    carried = (sides[1] * sides[2]).astype(BF16)
    carried_ref[...] = carried
    sent_ref[...] = carried.astype(F32).T.astype(BF16)


def short_forward(projected, before, taps):
    tok, _, cols = projected.shape
    side = jax.ShapeDtypeStruct((tok, cols), F32)
    return pl.pallas_call(
        pre_kernel,
        name="short_forward",
        out_shape=(
            side,
            side,
            side,
            jax.ShapeDtypeStruct((tok, cols), BF16),
            jax.ShapeDtypeStruct((cols, tok), BF16),
        ),
        cost_estimate=pl.CostEstimate(flops=5000000, bytes_accessed=3500000, transcendentals=0),
    )(projected.transpose(1, 0, 2), before.transpose(1, 0, 2), taps)


def channel_major(sent):
    count = lax.axis_size(SEQ)
    sent = sent.reshape(count, sent.shape[0] // count, sent.shape[1])
    return lax.all_to_all(sent, SEQ, split_axis=0, concat_axis=0, tiled=True)


def token_major(block):
    got = lax.all_to_all(block, SEQ, split_axis=0, concat_axis=0, tiled=True)
    return got.reshape(got.shape[0] * got.shape[1], got.shape[2])


def on_device(projected, short_weight, filters, skip, out_weight, cotangent):
    tok_rows, _ = cotangent.shape
    groups_dev, seq_length = filters.shape
    rim = SHORT - 1
    wide = lax.axis_size("x")
    yl, core = lax.axis_index("yl"), lax.axis_index("core")
    yh, x = lax.axis_index("yh"), lax.axis_index("x")
    steps = [(k, e) for k in range(wide) for e in range(2)]

    def scalars(sign):
        met = [((yh + e) % 2) * wide + (x + sign * k + wide) % wide for k, e in steps]
        return jnp.stack([yl, core] + met).astype(jnp.int32)

    before = from_behind(projected[tok_rows - rim :], 1)
    w_own = gathered(out_weight, "z", lax.axis_size("z"))
    cot_pair = jnp.stack([cotangent, swap(cotangent, "yh")])
    cots = [cot_pair] + [shift_x(cot_pair, k) for k in range(1, wide)]
    w_side = swap(w_own, "yl")
    w_own_other = swap(w_own, "core")
    w_side_other = swap(w_side, "core")
    ws = (w_own, w_own_other, w_side, w_side_other)

    tiles = toeplitz_tiles(filters.reshape(groups_dev, seq_length // HALF, HALF))
    query_side, key_side, value_side, carried, carried_sent = short_forward(
        projected, before, short_weight
    )
    carried_seq = channel_major(carried_sent)
    conv_seq = conv_forward(carried_seq, tiles)
    conv = token_major(conv_seq)

    gated_grad, mixed_grad, grad_sent = grad_matmul(scalars(-1), query_side, cots, ws)
    grad_seq = channel_major(grad_sent)

    parts, mixed_in = mix_matmul(scalars(1), conv, query_side, carried, skip, ws)
    shares = [parts[0]] + [shift_x(parts[k], k) for k in range(1, wide)]
    theirs = sum(p[1].astype(F32) for p in shares).astype(BF16)
    got = swap(theirs, "yh")
    mixed = (sum(p[0].astype(F32) for p in shares) + got.astype(F32)).astype(BF16)

    back_seq, filter_grad = conv_backward(grad_seq, carried_seq, tiles)
    back = token_major(back_seq).T
    query_grad = gated_grad * mixed_in
    carried_grad = back.astype(F32) + skip * mixed_grad.astype(F32)
    short_grad = jnp.stack([query_grad, carried_grad * value_side, carried_grad * key_side], axis=1)
    after = from_behind(short_grad[:rim], -1)
    extended_grad = jnp.concatenate([short_grad, after], axis=0)
    projected_grad = short_weight[:, 0, :] * extended_grad[rim : rim + tok_rows]
    for j in range(1, SHORT):
        projected_grad = (
            projected_grad
            + short_weight[:, j, :] * extended_grad[rim - j : rim - j + tok_rows]
        )
    return (mixed, projected_grad.astype(BF16), filter_grad.reshape(groups_dev, seq_length))


def solution(mesh):
    fine = Mesh(mesh.devices.reshape(8, 2, 2, 2, 4), ("z", "yl", "core", "yh", "x"))
    placed = (
        P(SEQ, None, CHAN),
        P(None, None, CHAN),
        P(CHAN + SEQ, None),
        P(CHAN),
        P(CHAN, SEQ),
        P(SEQ, CHAN),
    )
    return jax.shard_map(
        on_device,
        mesh=fine,
        in_specs=placed,
        out_specs=(P(SEQ, CHAN), P(SEQ, None, CHAN), P(CHAN + SEQ, None)),
        check_vma=False,
    )
```

```python
import functools
import math

import jax
import jax.numpy as jnp
from jax import lax
from jax.experimental import pallas as pl
from jax.experimental.pallas import tpu as pltpu
from jax.sharding import Mesh, PartitionSpec as P


GROUP = 8
SHORT = 3
BLOCK = 256
HALF = 128
LAGS = 4
WHALF = 4
BUILD_UNROLL = 16

SEQ = ("z", "yl", "core")
CHAN = ("yh", "x")
F32 = jnp.float32
BF16 = jnp.bfloat16


def from_behind(shard, by):
    count = lax.axis_size(SEQ)
    pairs = [(i, i + by) for i in range(count) if 0 <= i + by < count]
    return lax.ppermute(shard, SEQ, pairs)


def swap(shard, axis):
    return lax.ppermute(shard, axis, [(0, 1), (1, 0)])


def skew_masks():
    rows = lax.broadcasted_iota(jnp.int32, (HALF, HALF), 0)
    lanes = lax.broadcasted_iota(jnp.int32, (HALF, HALF), 1)
    return rows, lanes


def toeplitz_kernel(h_ref, tile_ref):
    groups, count, _ = h_ref.shape
    rows, lanes = skew_masks()
    inside = lanes >= rows
    for g in range(groups):
        tile_ref[g, 0] = jnp.zeros((HALF, HALF), BF16)

        def step(j, before, g=g):
            row = h_ref[g, pl.ds(j, 1), :]
            turned = pltpu.roll(jnp.broadcast_to(row, (HALF, HALF)), 0, 1, stride=1, stride_axis=0)
            tile_ref[g, j + 1] = jnp.where(inside, turned, before).astype(BF16)
            return turned

        lax.fori_loop(0, count, step, jnp.zeros((HALF, HALF), F32), unroll=BUILD_UNROLL)


def toeplitz_tiles(h):
    groups, count, _ = h.shape
    return pl.pallas_call(
        toeplitz_kernel,
        name="toeplitz_tiles",
        out_shape=jax.ShapeDtypeStruct((groups, count + 1, HALF, HALF), BF16),
        cost_estimate=pl.CostEstimate(flops=4000000, bytes_accessed=4500000, transcendentals=0),
    )(h)


def toeplitz_block(tile_ref, g, d):
    same = tile_ref[g, 2 * d + 1]
    upper = jnp.concatenate([same, tile_ref[g, 2 * d + 2]], axis=1)
    lower = jnp.concatenate([tile_ref[g, 2 * d], same], axis=1)
    return jnp.concatenate([upper, lower], axis=0)


def group_rows(ref, g):
    part = ref[...].astype(F32)[:, g * GROUP : (g + 1) * GROUP, :]
    return part.reshape(part.shape[0] * GROUP, BLOCK)


def conv_kernel(x_ref, tile_ref, y_ref, wide_ref, acc_ref):
    blocks, chans, _ = x_ref.shape
    total = blocks * GROUP
    parts = []
    for g in range(chans // GROUP):
        signal = group_rows(x_ref, g)
        for k in range(LAGS):
            late = signal
            if k > 0:
                late = jnp.concatenate(
                    [jnp.zeros((k * GROUP, BLOCK), F32), signal[: total - k * GROUP]], axis=0
                )
            wide_ref[:, k * BLOCK : (k + 1) * BLOCK] = late.astype(BF16)
        for d in range(0, blocks, LAGS):
            rows = total - d * GROUP
            weights = jnp.concatenate(
                [toeplitz_block(tile_ref, g, d + k) for k in range(LAGS)], axis=0
            )
            part = jnp.dot(wide_ref[:rows, :], weights, preferred_element_type=F32)
            if d == 0:
                acc_ref[...] = part
            else:
                acc_ref[d * GROUP :, :] += part
        parts.append(acc_ref[...].reshape(blocks, GROUP, BLOCK))
    y_ref[...] = jnp.concatenate(parts, axis=1).astype(BF16)


def back_kernel(m_ref, x_ref, tile_ref, y_ref, f_ref, wide_ref, acc_ref, low_ref, high_ref, *, scale):
    blocks, chans, _ = x_ref.shape
    total = blocks * GROUP
    rows_i, lanes_i = skew_masks()
    wrapped = lanes_i <= rows_i
    flip = (
        lax.broadcasted_iota(jnp.int32, (BLOCK, BLOCK), 0)
        + lax.broadcasted_iota(jnp.int32, (BLOCK, BLOCK), 1)
        == BLOCK - 1
    )
    flip = jnp.where(flip, 1.0, 0.0).astype(BF16)
    zero = jnp.zeros((HALF, HALF), F32)
    parts = []

    def fold(v):
        return v.reshape(HALF // 8, 8, HALF).sum(axis=0)

    def turned(cross, r, l):
        return pltpu.roll(
            cross[r * HALF : (r + 1) * HALF, l * HALF : (l + 1) * HALF], 1, 1, stride=1, stride_axis=0
        )

    for g in range(chans // GROUP):
        grad = group_rows(m_ref, g)
        wide_ref[total:, :] = jnp.zeros((wide_ref.shape[0] - total, LAGS * BLOCK), BF16)
        for k in range(LAGS):
            early = grad
            if k > 0:
                early = jnp.concatenate(
                    [grad[k * GROUP :], jnp.zeros((k * GROUP, BLOCK), F32)], axis=0
                )
            wide_ref[:total, k * BLOCK : (k + 1) * BLOCK] = early.astype(BF16)
        signal = group_rows(x_ref, g).astype(BF16)
        flipped = lax.dot_general(
            flip, signal, (((1,), (1,)), ((), ())), preferred_element_type=F32
        ).astype(BF16)
        high_ref[blocks] = jnp.zeros((8, BLOCK), F32)
        for d in range(0, blocks, LAGS):
            rows = total - d * GROUP
            weights = jnp.concatenate(
                [toeplitz_block(tile_ref, g, d + k) for k in range(LAGS)], axis=1
            )
            part = lax.dot_general(
                wide_ref[d * GROUP : total, :],
                weights,
                (((1,), (1,)), ((), ())),
                preferred_element_type=F32,
            )
            if d == 0:
                acc_ref[...] = part
            else:
                acc_ref[:rows, :] += part
            depth = total if 2 * d < blocks else total // 2
            cross_all = jnp.dot(
                flipped[:, :depth],
                wide_ref[d * GROUP : d * GROUP + depth, :],
                preferred_element_type=F32,
            )
            for k in range(LAGS):
                cross = cross_all[:, k * BLOCK : (k + 1) * BLOCK]
                s00, s01, s10, s11 = (turned(cross, r, l) for r in range(2) for l in range(2))
                low0 = jnp.where(wrapped, s01 + s10, s11)
                high0 = jnp.where(wrapped, zero, s00)
                low1 = jnp.where(wrapped, s11, zero)
                high1 = jnp.where(wrapped, s00, s01 + s10)
                low_ref[d + k] = jnp.concatenate([fold(low0), fold(low1)], axis=1)
                high_ref[d + k] = jnp.concatenate([fold(high0), fold(high1)], axis=1)
        parts.append(acc_ref[...].reshape(blocks, GROUP, BLOCK))
        f_ref[g] = (low_ref[...] + high_ref[pl.ds(1, blocks)]).sum(axis=1) * scale
    y_ref[...] = jnp.concatenate(parts, axis=1).astype(BF16)


def conv_forward(x, tiles):
    blocks = x.shape[0]
    total = blocks * GROUP
    return pl.pallas_call(
        conv_kernel,
        name="conv_forward",
        out_shape=jax.ShapeDtypeStruct(x.shape, BF16),
        scratch_shapes=[
            pltpu.VMEM((total, LAGS * BLOCK), BF16),
            pltpu.VMEM((total, BLOCK), F32),
        ],
        cost_estimate=pl.CostEstimate(flops=6000000000, bytes_accessed=600000, transcendentals=0),
    )(x, tiles)


def conv_backward(m, x, tiles):
    blocks, chans, _ = x.shape
    total = blocks * GROUP
    scale = 1.0 / math.sqrt(GROUP * blocks * BLOCK)
    return pl.pallas_call(
        functools.partial(back_kernel, scale=scale),
        name="conv_backward",
        out_shape=(
            jax.ShapeDtypeStruct(x.shape, BF16),
            jax.ShapeDtypeStruct((chans // GROUP, blocks, BLOCK), F32),
        ),
        scratch_shapes=[
            pltpu.VMEM((total + total // 2, LAGS * BLOCK), BF16),
            pltpu.VMEM((total, BLOCK), F32),
            pltpu.VMEM((blocks, 8, BLOCK), F32),
            pltpu.VMEM((blocks + 1, 8, BLOCK), F32),
        ],
        cost_estimate=pl.CostEstimate(flops=10000000000, bytes_accessed=1000000, transcendentals=0),
    )(m, x, tiles)


def whole_columns(at_ref, sign, step, refs):
    own, own_c, side, side_c, own2, own_c2, side2, side_c2 = refs
    first = at_ref[1] == 0
    met = ((at_ref[2] + step) & 1) * 4 + ((at_ref[3] + sign * (step // 2) + 4) & 3)
    place = (at_ref[4] - met + 9) & 7
    early = place < WHALF
    lo = jnp.minimum(place, WHALF - 1)
    hi = jnp.maximum(place - WHALF, 0)

    def pick(a, b):
        return jnp.where(early, a[lo], b[hi])

    parts = []
    for a, b, c, d in ((own, own2, own_c, own_c2), (side, side2, side_c, side_c2)):
        mine, other = pick(a, b), pick(c, d)
        parts += [jnp.where(first, mine, other), jnp.where(first, other, mine)]
    return jnp.concatenate(parts, axis=1)


def side_columns(side, width):
    return pl.ds(pl.multiple_of(side * width, width), width)


def grad_mm_kernel(at_ref, query_ref, cot0, cot1, cot2, cot3, *refs):
    *w_refs, out_ref, mixed_ref, sent_ref = refs
    yl = at_ref[0]
    width = cot0.shape[2] // 2
    for step in range(8):
        cot_ref = (cot0, cot1, cot2, cot3)[step // 2]
        e = step % 2
        lhs = jnp.concatenate(
            [cot_ref[e, :, side_columns(yl, width)], cot_ref[e, :, side_columns(1 - yl, width)]],
            axis=1,
        )
        part = lax.dot_general(
            lhs,
            whole_columns(at_ref, -1, step, w_refs),
            (((1,), (1,)), ((), ())),
            preferred_element_type=F32,
        )
        if step == 0:
            out_ref[...] = part
        else:
            out_ref[...] += part
    mixed = (out_ref[...] * query_ref[...]).astype(BF16)
    mixed_ref[...] = mixed
    sent_ref[...] = mixed.astype(F32).T.astype(BF16)


SCALARS = pl.BlockSpec(memory_space=pltpu.SMEM)
WHOLE = pl.BlockSpec(memory_space=pltpu.VMEM)


def grad_matmul(at, query, cots, ws):
    tok, rows = query.shape
    return pl.pallas_call(
        grad_mm_kernel,
        name="grad_matmul",
        out_shape=(
            jax.ShapeDtypeStruct((tok, rows), F32),
            jax.ShapeDtypeStruct((tok, rows), BF16),
            jax.ShapeDtypeStruct((rows, tok), BF16),
        ),
        in_specs=[SCALARS] + [WHOLE] * (1 + len(cots) + len(ws)),
        out_specs=(WHOLE,) * 3,
        cost_estimate=pl.CostEstimate(flops=4000000000, bytes_accessed=6500000, transcendentals=0),
    )(at, query, *cots, *ws)


def mix_mm_kernel(at_ref, conv_ref, query_ref, carried_ref, skip_ref, *refs):
    *w_refs, out0, out1, out2, out3, mixed_ref = refs
    yl = at_ref[0]
    conv = conv_ref[...].astype(F32).T
    mixed_in = conv + skip_ref[...] * carried_ref[...].astype(F32)
    mixed_ref[...] = mixed_in
    gated = (query_ref[...] * mixed_in).astype(BF16)
    width = out0.shape[2] // 2
    for step in range(8):
        out_ref = (out0, out1, out2, out3)[step // 2]
        e = step % 2
        part = jnp.dot(
            gated, whole_columns(at_ref, 1, step, w_refs), preferred_element_type=F32
        ).astype(BF16)
        out_ref[e, :, side_columns(yl, width)] = part[:, :width]
        out_ref[e, :, side_columns(1 - yl, width)] = part[:, width:]


def mix_matmul(at, conv, query, carried, skip, ws):
    tok, rows = query.shape
    cols = 4 * ws[0].shape[2]
    *parts, mixed_in = pl.pallas_call(
        mix_mm_kernel,
        name="mix_matmul",
        out_shape=(jax.ShapeDtypeStruct((2, tok, cols), BF16),) * 4
        + (jax.ShapeDtypeStruct((tok, rows), F32),),
        in_specs=[SCALARS] + [WHOLE] * (4 + len(ws)),
        out_specs=(WHOLE,) * 5,
        cost_estimate=pl.CostEstimate(flops=4000000000, bytes_accessed=6500000, transcendentals=0),
    )(at, conv, query, carried, skip[None, :], *ws)
    return parts, mixed_in


def shift_z(shard, by):
    count = lax.axis_size("z")
    return lax.ppermute(shard, "z", [(i, (i + by) % count) for i in range(count)])


def shift_x(shard, by):
    count = lax.axis_size("x")
    return lax.ppermute(shard, "x", [(i, (i + by) % count) for i in range(count)])


def pre_kernel(proj_ref, before_ref, taps_ref, query_ref, key_ref, value_ref, carried_ref, sent_ref):
    row = lax.broadcasted_iota(jnp.int32, proj_ref.shape[1:], 0)
    sides = []
    for i in range(3):
        now = proj_ref[i].astype(F32)
        before = before_ref[i].astype(F32)
        total = taps_ref[i, SHORT - 1 : SHORT, :] * now
        for j in range(1, SHORT):
            late = pltpu.roll(now, j, 0)
            for r in range(j):
                late = jnp.where(row == r, before[SHORT - 1 - j + r][None, :], late)
            total = total + taps_ref[i, SHORT - 1 - j : SHORT - j, :] * late
        sides.append(total)
    query_ref[...], key_ref[...], value_ref[...] = sides
    carried = (sides[1] * sides[2]).astype(BF16)
    carried_ref[...] = carried
    sent_ref[...] = carried.astype(F32).T.astype(BF16)


def short_forward(projected, before, taps):
    tok, _, cols = projected.shape
    side = jax.ShapeDtypeStruct((tok, cols), F32)
    return pl.pallas_call(
        pre_kernel,
        name="short_forward",
        out_shape=(
            side,
            side,
            side,
            jax.ShapeDtypeStruct((tok, cols), BF16),
            jax.ShapeDtypeStruct((cols, tok), BF16),
        ),
        cost_estimate=pl.CostEstimate(flops=5000000, bytes_accessed=3500000, transcendentals=0),
    )(projected.transpose(1, 0, 2), before.transpose(1, 0, 2), taps)


def channel_major(sent):
    count = lax.axis_size(SEQ)
    sent = sent.reshape(count, sent.shape[0] // count, sent.shape[1])
    return lax.all_to_all(sent, SEQ, split_axis=0, concat_axis=0, tiled=True)


def token_major(block):
    got = lax.all_to_all(block, SEQ, split_axis=0, concat_axis=0, tiled=True)
    return got.reshape(got.shape[0] * got.shape[1], got.shape[2])


def on_device(projected, short_weight, filters, skip, out_weight, cotangent):
    tok_rows, _ = cotangent.shape
    groups_dev, seq_length = filters.shape
    rim = SHORT - 1
    wide, deep = lax.axis_size("x"), lax.axis_size("z")
    yl, core = lax.axis_index("yl"), lax.axis_index("core")
    yh, x, z = lax.axis_index("yh"), lax.axis_index("x"), lax.axis_index("z")

    at = jnp.stack([yl, core, yh, x, z]).astype(jnp.int32)
    before = from_behind(projected[tok_rows - rim :], 1)
    cot_pair = jnp.stack([cotangent, swap(cotangent, "yh")])
    cots = [cot_pair] + [shift_x(cot_pair, k) for k in range(1, wide)]
    w_own = jnp.stack(
        [shift_z(out_weight, deep - 1), out_weight, shift_z(out_weight, 1), shift_z(out_weight, 2)]
    )
    w_own2 = jnp.stack([shift_z(out_weight, r) for r in range(3, deep - 1)])
    w_side = swap(w_own, "yl")
    w_side2 = swap(w_own2, "yl")
    w_own_c = swap(w_own, "core")
    w_side_c = swap(w_side, "core")
    w_own_c2 = swap(w_own2, "core")
    w_side_c2 = swap(w_side2, "core")
    ws = (w_own, w_own_c, w_side, w_side_c, w_own2, w_own_c2, w_side2, w_side_c2)

    tiles = toeplitz_tiles(filters.reshape(groups_dev, seq_length // HALF, HALF))
    query_side, key_side, value_side, carried, carried_sent = short_forward(
        projected, before, short_weight
    )
    carried_seq = channel_major(carried_sent)
    conv_seq = conv_forward(carried_seq, tiles)
    conv = token_major(conv_seq)

    gated_grad, mixed_grad, grad_sent = grad_matmul(at, query_side, cots, ws)
    grad_seq = channel_major(grad_sent)

    parts, mixed_in = mix_matmul(at, conv, query_side, carried, skip, ws)
    shares = [parts[0]] + [shift_x(parts[k], k) for k in range(1, wide)]
    theirs = sum(p[1].astype(F32) for p in shares).astype(BF16)
    got = swap(theirs, "yh")
    mixed = (sum(p[0].astype(F32) for p in shares) + got.astype(F32)).astype(BF16)

    back_seq, filter_grad = conv_backward(grad_seq, carried_seq, tiles)
    back = token_major(back_seq).T
    query_grad = gated_grad * mixed_in
    carried_grad = back.astype(F32) + skip * mixed_grad.astype(F32)
    short_grad = jnp.stack([query_grad, carried_grad * value_side, carried_grad * key_side], axis=1)
    after = from_behind(short_grad[:rim], -1)
    extended_grad = jnp.concatenate([short_grad, after], axis=0)
    projected_grad = short_weight[:, 0, :] * extended_grad[rim : rim + tok_rows]
    for j in range(1, SHORT):
        projected_grad = (
            projected_grad
            + short_weight[:, j, :] * extended_grad[rim - j : rim - j + tok_rows]
        )
    return (mixed, projected_grad.astype(BF16), filter_grad.reshape(groups_dev, seq_length))


def solution(mesh):
    fine = Mesh(mesh.devices.reshape(8, 2, 2, 2, 4), ("z", "yl", "core", "yh", "x"))
    placed = (
        P(SEQ, None, CHAN),
        P(None, None, CHAN),
        P(CHAN + SEQ, None),
        P(CHAN),
        P(CHAN, SEQ),
        P(SEQ, CHAN),
    )
    return jax.shard_map(
        on_device,
        mesh=fine,
        in_specs=placed,
        out_specs=(P(SEQ, CHAN), P(SEQ, None, CHAN), P(CHAN + SEQ, None)),
        check_vma=False,
    )
```

```python
import functools
import math

import jax
import jax.numpy as jnp
from jax import lax
from jax.experimental import pallas as pl
from jax.experimental.pallas import tpu as pltpu
from jax.sharding import Mesh, PartitionSpec as P


GROUP = 8
SHORT = 3
BLOCK = 256
HALF = 128
LAGS = 4
WHALF = 4
SCRATCH = pltpu.CompilerParams(vmem_limit_bytes=24 << 20)
BUILD_UNROLL = 16

SEQ = ("z", "yl", "core")
CHAN = ("yh", "x")
F32 = jnp.float32
BF16 = jnp.bfloat16


def from_behind(shard, by):
    count = lax.axis_size(SEQ)
    pairs = [(i, i + by) for i in range(count) if 0 <= i + by < count]
    return lax.ppermute(shard, SEQ, pairs)


def swap(shard, axis):
    return lax.ppermute(shard, axis, [(0, 1), (1, 0)])


def skew_masks():
    rows = lax.broadcasted_iota(jnp.int32, (HALF, HALF), 0)
    lanes = lax.broadcasted_iota(jnp.int32, (HALF, HALF), 1)
    return rows, lanes


def toeplitz_kernel(h_ref, tile_ref):
    groups, count = tile_ref.shape[0], tile_ref.shape[1] - 1
    rows, lanes = skew_masks()
    inside = lanes >= rows
    zero = jnp.zeros((HALF, HALF), F32)
    for g in range(groups):
        tile_ref[g, 0] = zero.astype(BF16)

    def step(j, before):
        turns = []
        for g in range(groups):
            row = h_ref[g : g + 1, pl.ds(pl.multiple_of(j * HALF, HALF), HALF)]
            turned = pltpu.roll(jnp.broadcast_to(row, (HALF, HALF)), 0, 1, stride=1, stride_axis=0)
            tile_ref[g, j + 1] = jnp.where(inside, turned, before[g]).astype(BF16)
            turns.append(turned)
        return tuple(turns)

    lax.fori_loop(0, count, step, (zero,) * groups, unroll=BUILD_UNROLL)


def toeplitz_tiles(h):
    groups, length = h.shape
    return pl.pallas_call(
        toeplitz_kernel,
        name="toeplitz_tiles",
        out_shape=pltpu.VMEM((groups, length // HALF + 1, HALF, HALF), BF16),
        compiler_params=SCRATCH,
        cost_estimate=pl.CostEstimate(flops=4000000, bytes_accessed=4500000, transcendentals=0),
    )(h)


def toeplitz_block(tile_ref, g, d):
    same = tile_ref[g, 2 * d + 1]
    upper = jnp.concatenate([same, tile_ref[g, 2 * d + 2]], axis=1)
    lower = jnp.concatenate([tile_ref[g, 2 * d], same], axis=1)
    return jnp.concatenate([upper, lower], axis=0)


def group_rows(ref, g):
    part = ref[...].astype(F32)[:, g * GROUP : (g + 1) * GROUP, :]
    return part.reshape(part.shape[0] * GROUP, BLOCK)


def conv_kernel(x_ref, tile_ref, y_ref, wide_ref, acc_ref):
    blocks, chans, _ = x_ref.shape
    total = blocks * GROUP
    parts = []
    for g in range(chans // GROUP):
        signal = group_rows(x_ref, g)
        for k in range(LAGS):
            late = signal
            if k > 0:
                late = jnp.concatenate(
                    [jnp.zeros((k * GROUP, BLOCK), F32), signal[: total - k * GROUP]], axis=0
                )
            wide_ref[:, k * BLOCK : (k + 1) * BLOCK] = late.astype(BF16)
        for d in range(0, blocks, LAGS):
            rows = total - d * GROUP
            weights = jnp.concatenate(
                [toeplitz_block(tile_ref, g, d + k) for k in range(LAGS)], axis=0
            )
            part = jnp.dot(wide_ref[:rows, :], weights, preferred_element_type=F32)
            if d == 0:
                acc_ref[...] = part
            else:
                acc_ref[d * GROUP :, :] += part
        parts.append(acc_ref[...].reshape(blocks, GROUP, BLOCK))
    y_ref[...] = jnp.concatenate(parts, axis=1).astype(BF16)


def back_kernel(m_ref, x_ref, tile_ref, y_ref, f_ref, wide_ref, acc_ref, low_ref, high_ref, *, scale):
    blocks, chans, _ = x_ref.shape
    total = blocks * GROUP
    rows_i, lanes_i = skew_masks()
    wrapped = lanes_i <= rows_i
    flip = (
        lax.broadcasted_iota(jnp.int32, (BLOCK, BLOCK), 0)
        + lax.broadcasted_iota(jnp.int32, (BLOCK, BLOCK), 1)
        == BLOCK - 1
    )
    flip = jnp.where(flip, 1.0, 0.0).astype(BF16)
    zero = jnp.zeros((HALF, HALF), F32)
    parts = []

    def fold(v):
        return v.reshape(HALF // 8, 8, HALF).sum(axis=0)

    def turned(cross, r, l):
        return pltpu.roll(
            cross[r * HALF : (r + 1) * HALF, l * HALF : (l + 1) * HALF], 1, 1, stride=1, stride_axis=0
        )

    for g in range(chans // GROUP):
        grad = group_rows(m_ref, g)
        wide_ref[total:, :] = jnp.zeros((wide_ref.shape[0] - total, LAGS * BLOCK), BF16)
        for k in range(LAGS):
            early = grad
            if k > 0:
                early = jnp.concatenate(
                    [grad[k * GROUP :], jnp.zeros((k * GROUP, BLOCK), F32)], axis=0
                )
            wide_ref[:total, k * BLOCK : (k + 1) * BLOCK] = early.astype(BF16)
        signal = group_rows(x_ref, g).astype(BF16)
        flipped = lax.dot_general(
            flip, signal, (((1,), (1,)), ((), ())), preferred_element_type=F32
        ).astype(BF16)
        high_ref[blocks] = jnp.zeros((8, BLOCK), F32)
        for d in range(0, blocks, LAGS):
            rows = total - d * GROUP
            weights = jnp.concatenate(
                [toeplitz_block(tile_ref, g, d + k) for k in range(LAGS)], axis=1
            )
            part = lax.dot_general(
                wide_ref[d * GROUP : total, :],
                weights,
                (((1,), (1,)), ((), ())),
                preferred_element_type=F32,
            )
            if d == 0:
                acc_ref[...] = part
            else:
                acc_ref[:rows, :] += part
            depth = total if 2 * d < blocks else total // 2
            cross_all = jnp.dot(
                flipped[:, :depth],
                wide_ref[d * GROUP : d * GROUP + depth, :],
                preferred_element_type=F32,
            )
            for k in range(LAGS):
                cross = cross_all[:, k * BLOCK : (k + 1) * BLOCK]
                s00, s01, s10, s11 = (turned(cross, r, l) for r in range(2) for l in range(2))
                low0 = jnp.where(wrapped, s01 + s10, s11)
                high0 = jnp.where(wrapped, zero, s00)
                low1 = jnp.where(wrapped, s11, zero)
                high1 = jnp.where(wrapped, s00, s01 + s10)
                low_ref[d + k] = jnp.concatenate([fold(low0), fold(low1)], axis=1)
                high_ref[d + k] = jnp.concatenate([fold(high0), fold(high1)], axis=1)
        parts.append(acc_ref[...].reshape(blocks, GROUP, BLOCK))
        f_ref[g] = (low_ref[...] + high_ref[pl.ds(1, blocks)]).sum(axis=1) * scale
    y_ref[...] = jnp.concatenate(parts, axis=1).astype(BF16)


def conv_forward(x, tiles):
    blocks = x.shape[0]
    total = blocks * GROUP
    return pl.pallas_call(
        conv_kernel,
        name="conv_forward",
        out_shape=jax.ShapeDtypeStruct(x.shape, BF16),
        scratch_shapes=[
            pltpu.VMEM((total, LAGS * BLOCK), BF16),
            pltpu.VMEM((total, BLOCK), F32),
        ],
        compiler_params=SCRATCH,
        cost_estimate=pl.CostEstimate(flops=6000000000, bytes_accessed=600000, transcendentals=0),
    )(x, pltpu.with_memory_space_constraint(tiles, pltpu.VMEM))


def conv_backward(m, x, tiles):
    blocks, chans, _ = x.shape
    total = blocks * GROUP
    scale = 1.0 / math.sqrt(GROUP * blocks * BLOCK)
    return pl.pallas_call(
        functools.partial(back_kernel, scale=scale),
        name="conv_backward",
        out_shape=(
            jax.ShapeDtypeStruct(x.shape, BF16),
            jax.ShapeDtypeStruct((chans // GROUP, blocks, BLOCK), F32),
        ),
        scratch_shapes=[
            pltpu.VMEM((total + total // 2, LAGS * BLOCK), BF16),
            pltpu.VMEM((total, BLOCK), F32),
            pltpu.VMEM((blocks, 8, BLOCK), F32),
            pltpu.VMEM((blocks + 1, 8, BLOCK), F32),
        ],
        compiler_params=SCRATCH,
        cost_estimate=pl.CostEstimate(flops=10000000000, bytes_accessed=1000000, transcendentals=0),
    )(m, x, pltpu.with_memory_space_constraint(tiles, pltpu.VMEM))


def whole_columns(at_ref, sign, step, refs):
    own, own_c, side, side_c, own2, own_c2, side2, side_c2 = refs
    first = at_ref[1] == 0
    met = ((at_ref[2] + step) & 1) * 4 + ((at_ref[3] + sign * (step // 2) + 4) & 3)
    place = (at_ref[4] - met + 9) & 7
    early = place < WHALF
    lo = jnp.minimum(place, WHALF - 1)
    hi = jnp.maximum(place - WHALF, 0)

    def pick(a, b):
        return jnp.where(early, a[lo], b[hi])

    parts = []
    for a, b, c, d in ((own, own2, own_c, own_c2), (side, side2, side_c, side_c2)):
        mine, other = pick(a, b), pick(c, d)
        parts += [jnp.where(first, mine, other), jnp.where(first, other, mine)]
    return jnp.concatenate(parts, axis=1)


def side_columns(side, width):
    return pl.ds(pl.multiple_of(side * width, width), width)


def grad_mm_kernel(at_ref, query_ref, cot0, cot1, cot2, cot3, *refs):
    *w_refs, out_ref, mixed_ref, sent_ref = refs
    yl = at_ref[0]
    width = cot0.shape[2] // 2
    for step in range(8):
        cot_ref = (cot0, cot1, cot2, cot3)[step // 2]
        e = step % 2
        lhs = jnp.concatenate(
            [cot_ref[e, :, side_columns(yl, width)], cot_ref[e, :, side_columns(1 - yl, width)]],
            axis=1,
        )
        part = lax.dot_general(
            lhs,
            whole_columns(at_ref, -1, step, w_refs),
            (((1,), (1,)), ((), ())),
            preferred_element_type=F32,
        )
        if step == 0:
            out_ref[...] = part
        else:
            out_ref[...] += part
    mixed = (out_ref[...] * query_ref[...]).astype(BF16)
    mixed_ref[...] = mixed
    sent_ref[...] = mixed.astype(F32).T.astype(BF16)


SCALARS = pl.BlockSpec(memory_space=pltpu.SMEM)
WHOLE = pl.BlockSpec(memory_space=pltpu.VMEM)


def grad_matmul(at, query, cots, ws):
    tok, rows = query.shape
    return pl.pallas_call(
        grad_mm_kernel,
        name="grad_matmul",
        out_shape=(
            jax.ShapeDtypeStruct((tok, rows), F32),
            jax.ShapeDtypeStruct((tok, rows), BF16),
            jax.ShapeDtypeStruct((rows, tok), BF16),
        ),
        in_specs=[SCALARS] + [WHOLE] * (1 + len(cots) + len(ws)),
        out_specs=(WHOLE,) * 3,
        compiler_params=SCRATCH,
        cost_estimate=pl.CostEstimate(flops=4000000000, bytes_accessed=6500000, transcendentals=0),
    )(at, query, *cots, *ws)


def mix_mm_kernel(at_ref, conv_ref, query_ref, carried_ref, skip_ref, *refs):
    *w_refs, out0, out1, out2, out3, mixed_ref = refs
    yl = at_ref[0]
    conv = conv_ref[...].astype(F32).T
    mixed_in = conv + skip_ref[...] * carried_ref[...].astype(F32)
    mixed_ref[...] = mixed_in
    gated = (query_ref[...] * mixed_in).astype(BF16)
    width = out0.shape[2] // 2
    for step in range(8):
        out_ref = (out0, out1, out2, out3)[step // 2]
        e = step % 2
        part = jnp.dot(
            gated, whole_columns(at_ref, 1, step, w_refs), preferred_element_type=F32
        ).astype(BF16)
        out_ref[e, :, side_columns(yl, width)] = part[:, :width]
        out_ref[e, :, side_columns(1 - yl, width)] = part[:, width:]


def mix_matmul(at, conv, query, carried, skip, ws):
    tok, rows = query.shape
    cols = 4 * ws[0].shape[2]
    *parts, mixed_in = pl.pallas_call(
        mix_mm_kernel,
        name="mix_matmul",
        out_shape=(jax.ShapeDtypeStruct((2, tok, cols), BF16),) * 4
        + (jax.ShapeDtypeStruct((tok, rows), F32),),
        in_specs=[SCALARS] + [WHOLE] * (4 + len(ws)),
        out_specs=(WHOLE,) * 5,
        compiler_params=SCRATCH,
        cost_estimate=pl.CostEstimate(flops=4000000000, bytes_accessed=6500000, transcendentals=0),
    )(at, conv, query, carried, skip[None, :], *ws)
    return parts, mixed_in


def shift_z(shard, by):
    count = lax.axis_size("z")
    return lax.ppermute(shard, "z", [(i, (i + by) % count) for i in range(count)])


def shift_x(shard, by):
    count = lax.axis_size("x")
    return lax.ppermute(shard, "x", [(i, (i + by) % count) for i in range(count)])


def pre_kernel(proj_ref, before_ref, taps_ref, query_ref, key_ref, value_ref, carried_ref, sent_ref):
    row = lax.broadcasted_iota(jnp.int32, proj_ref.shape[1:], 0)
    sides = []
    for i in range(3):
        now = proj_ref[i].astype(F32)
        before = before_ref[i].astype(F32)
        total = taps_ref[i, SHORT - 1 : SHORT, :] * now
        for j in range(1, SHORT):
            late = pltpu.roll(now, j, 0)
            for r in range(j):
                late = jnp.where(row == r, before[SHORT - 1 - j + r][None, :], late)
            total = total + taps_ref[i, SHORT - 1 - j : SHORT - j, :] * late
        sides.append(total)
    query_ref[...], key_ref[...], value_ref[...] = sides
    carried = (sides[1] * sides[2]).astype(BF16)
    carried_ref[...] = carried
    sent_ref[...] = carried.astype(F32).T.astype(BF16)


def short_forward(projected, before, taps):
    tok, _, cols = projected.shape
    side = jax.ShapeDtypeStruct((tok, cols), F32)
    return pl.pallas_call(
        pre_kernel,
        name="short_forward",
        out_shape=(
            side,
            side,
            side,
            jax.ShapeDtypeStruct((tok, cols), BF16),
            jax.ShapeDtypeStruct((cols, tok), BF16),
        ),
        compiler_params=SCRATCH,
        cost_estimate=pl.CostEstimate(flops=5000000, bytes_accessed=3500000, transcendentals=0),
    )(projected.transpose(1, 0, 2), before.transpose(1, 0, 2), taps)


def channel_major(sent):
    count = lax.axis_size(SEQ)
    sent = sent.reshape(count, sent.shape[0] // count, sent.shape[1])
    return lax.all_to_all(sent, SEQ, split_axis=0, concat_axis=0, tiled=True)


def token_major(block):
    got = lax.all_to_all(block, SEQ, split_axis=0, concat_axis=0, tiled=True)
    return got.reshape(got.shape[0] * got.shape[1], got.shape[2])


def on_device(projected, short_weight, filters, skip, out_weight, cotangent):
    tok_rows, _ = cotangent.shape
    groups_dev, seq_length = filters.shape
    rim = SHORT - 1
    wide, deep = lax.axis_size("x"), lax.axis_size("z")
    yl, core = lax.axis_index("yl"), lax.axis_index("core")
    yh, x, z = lax.axis_index("yh"), lax.axis_index("x"), lax.axis_index("z")

    at = jnp.stack([yl, core, yh, x, z]).astype(jnp.int32)
    before = from_behind(projected[tok_rows - rim :], 1)
    cot_pair = jnp.stack([cotangent, swap(cotangent, "yh")])
    cots = [cot_pair] + [shift_x(cot_pair, k) for k in range(1, wide)]
    w_own = jnp.stack(
        [shift_z(out_weight, deep - 1), out_weight, shift_z(out_weight, 1), shift_z(out_weight, 2)]
    )
    w_own2 = jnp.stack([shift_z(out_weight, r) for r in range(3, deep - 1)])
    w_side = swap(w_own, "yl")
    w_side2 = swap(w_own2, "yl")
    w_own_c = swap(w_own, "core")
    w_side_c = swap(w_side, "core")
    w_own_c2 = swap(w_own2, "core")
    w_side_c2 = swap(w_side2, "core")
    ws = (w_own, w_own_c, w_side, w_side_c, w_own2, w_own_c2, w_side2, w_side_c2)

    tiles = toeplitz_tiles(filters)
    query_side, key_side, value_side, carried, carried_sent = short_forward(
        projected, before, short_weight
    )
    carried_seq = channel_major(carried_sent)
    conv_seq = conv_forward(carried_seq, tiles)
    conv = token_major(conv_seq)

    gated_grad, mixed_grad, grad_sent = grad_matmul(at, query_side, cots, ws)
    grad_seq = channel_major(grad_sent)

    parts, mixed_in = mix_matmul(at, conv, query_side, carried, skip, ws)
    shares = [parts[0]] + [shift_x(parts[k], k) for k in range(1, wide)]
    theirs = sum(p[1].astype(F32) for p in shares).astype(BF16)
    got = swap(theirs, "yh")
    mixed = (sum(p[0].astype(F32) for p in shares) + got.astype(F32)).astype(BF16)

    back_seq, filter_grad = conv_backward(grad_seq, carried_seq, tiles)
    back = token_major(back_seq).T
    query_grad = gated_grad * mixed_in
    carried_grad = back.astype(F32) + skip * mixed_grad.astype(F32)
    short_grad = jnp.stack([query_grad, carried_grad * value_side, carried_grad * key_side], axis=1)
    after = from_behind(short_grad[:rim], -1)
    extended_grad = jnp.concatenate([short_grad, after], axis=0)
    projected_grad = short_weight[:, 0, :] * extended_grad[rim : rim + tok_rows]
    for j in range(1, SHORT):
        projected_grad = (
            projected_grad
            + short_weight[:, j, :] * extended_grad[rim - j : rim - j + tok_rows]
        )
    return (mixed, projected_grad.astype(BF16), filter_grad.reshape(groups_dev, seq_length))


def solution(mesh):
    fine = Mesh(mesh.devices.reshape(8, 2, 2, 2, 4), ("z", "yl", "core", "yh", "x"))
    placed = (
        P(SEQ, None, CHAN),
        P(None, None, CHAN),
        P(CHAN + SEQ, None),
        P(CHAN),
        P(CHAN, SEQ),
        P(SEQ, CHAN),
    )
    return jax.shard_map(
        on_device,
        mesh=fine,
        in_specs=placed,
        out_specs=(P(SEQ, CHAN), P(SEQ, None, CHAN), P(CHAN + SEQ, None)),
        check_vma=False,
    )
```

```python
import functools
import math

import jax
import jax.numpy as jnp
from jax import lax
from jax.experimental import pallas as pl
from jax.experimental.pallas import tpu as pltpu
from jax.sharding import Mesh, PartitionSpec as P


GROUP = 8
SHORT = 3
BLOCK = 256
HALF = 128
LAGS = 4
SCRATCH = pltpu.CompilerParams(vmem_limit_bytes=24 << 20)
BUILD_UNROLL = 16
EDGE = 16
OUTSIDE = pltpu.HBM

SEQ = ("z", "yl", "core")
CHAN = ("yh", "x")
F32 = jnp.float32
BF16 = jnp.bfloat16


def from_behind(shard, by):
    count = lax.axis_size(SEQ)
    pairs = [(i, i + by) for i in range(count) if 0 <= i + by < count]
    return lax.ppermute(shard, SEQ, pairs)


def swap(shard, axis):
    return lax.ppermute(shard, axis, [(0, 1), (1, 0)])


def skew_masks():
    rows = lax.broadcasted_iota(jnp.int32, (HALF, HALF), 0)
    lanes = lax.broadcasted_iota(jnp.int32, (HALF, HALF), 1)
    return rows, lanes


def build_tiles(h_ref, tile_ref):
    groups, count = tile_ref.shape[0], tile_ref.shape[1] - 1
    rows, lanes = skew_masks()
    inside = lanes >= rows
    zero = jnp.zeros((HALF, HALF), F32)
    for g in range(groups):
        tile_ref[g, 0] = zero.astype(BF16)

    def step(j, before):
        turns = []
        for g in range(groups):
            row = h_ref[g : g + 1, pl.ds(pl.multiple_of(j * HALF, HALF), HALF)]
            turned = pltpu.roll(jnp.broadcast_to(row, (HALF, HALF)), 0, 1, stride=1, stride_axis=0)
            tile_ref[g, j + 1] = jnp.where(inside, turned, before[g]).astype(BF16)
            turns.append(turned)
        return tuple(turns)

    lax.fori_loop(0, count, step, (zero,) * groups, unroll=BUILD_UNROLL)


def toeplitz_block(tile_ref, g, d):
    same = tile_ref[g, 2 * d + 1]
    upper = jnp.concatenate([same, tile_ref[g, 2 * d + 2]], axis=1)
    lower = jnp.concatenate([tile_ref[g, 2 * d], same], axis=1)
    return jnp.concatenate([upper, lower], axis=0)


def group_rows(ref, g):
    part = ref[...].astype(F32)[:, g * GROUP : (g + 1) * GROUP, :]
    return part.reshape(part.shape[0] * GROUP, BLOCK)


def conv_kernel(x_ref, h_ref, y_ref, tile_ref, wide_ref, acc_ref):
    blocks, chans, _ = x_ref.shape
    total = blocks * GROUP
    parts = []
    build_tiles(h_ref, tile_ref)
    for g in range(chans // GROUP):
        signal = group_rows(x_ref, g)
        for k in range(LAGS):
            late = signal
            if k > 0:
                late = jnp.concatenate(
                    [jnp.zeros((k * GROUP, BLOCK), F32), signal[: total - k * GROUP]], axis=0
                )
            wide_ref[:, k * BLOCK : (k + 1) * BLOCK] = late.astype(BF16)
        for d in range(0, blocks, LAGS):
            rows = total - d * GROUP
            weights = jnp.concatenate(
                [toeplitz_block(tile_ref, g, d + k) for k in range(LAGS)], axis=0
            )
            part = jnp.dot(wide_ref[:rows, :], weights, preferred_element_type=F32)
            if d == 0:
                acc_ref[...] = part
            else:
                acc_ref[d * GROUP :, :] += part
        parts.append(acc_ref[...].reshape(blocks, GROUP, BLOCK))
    y_ref[...] = jnp.concatenate(parts, axis=1).astype(BF16)


def back_kernel(m_ref, x_ref, h_ref, y_ref, f_ref, tile_ref, wide_ref, acc_ref, low_ref, high_ref, *, scale):
    blocks, chans, _ = x_ref.shape
    total = blocks * GROUP
    rows_i, lanes_i = skew_masks()
    wrapped = lanes_i <= rows_i
    flip = (
        lax.broadcasted_iota(jnp.int32, (BLOCK, BLOCK), 0)
        + lax.broadcasted_iota(jnp.int32, (BLOCK, BLOCK), 1)
        == BLOCK - 1
    )
    flip = jnp.where(flip, 1.0, 0.0).astype(BF16)
    zero = jnp.zeros((HALF, HALF), F32)
    build_tiles(h_ref, tile_ref)
    parts = []

    def fold(v):
        return v.reshape(HALF // 8, 8, HALF).sum(axis=0)

    def turned(cross, r, l):
        return pltpu.roll(
            cross[r * HALF : (r + 1) * HALF, l * HALF : (l + 1) * HALF], 1, 1, stride=1, stride_axis=0
        )

    for g in range(chans // GROUP):
        grad = group_rows(m_ref, g)
        wide_ref[total:, :] = jnp.zeros((wide_ref.shape[0] - total, LAGS * BLOCK), BF16)
        for k in range(LAGS):
            early = grad
            if k > 0:
                early = jnp.concatenate(
                    [grad[k * GROUP :], jnp.zeros((k * GROUP, BLOCK), F32)], axis=0
                )
            wide_ref[:total, k * BLOCK : (k + 1) * BLOCK] = early.astype(BF16)
        signal = group_rows(x_ref, g).astype(BF16)
        flipped = lax.dot_general(
            flip, signal, (((1,), (1,)), ((), ())), preferred_element_type=F32
        ).astype(BF16)
        high_ref[blocks] = jnp.zeros((8, BLOCK), F32)
        for d in range(0, blocks, LAGS):
            rows = total - d * GROUP
            weights = jnp.concatenate(
                [toeplitz_block(tile_ref, g, d + k) for k in range(LAGS)], axis=1
            )
            part = lax.dot_general(
                wide_ref[d * GROUP : total, :],
                weights,
                (((1,), (1,)), ((), ())),
                preferred_element_type=F32,
            )
            if d == 0:
                acc_ref[...] = part
            else:
                acc_ref[:rows, :] += part
            depth = total if 2 * d < blocks else total // 2
            cross_all = jnp.dot(
                flipped[:, :depth],
                wide_ref[d * GROUP : d * GROUP + depth, :],
                preferred_element_type=F32,
            )
            for k in range(LAGS):
                cross = cross_all[:, k * BLOCK : (k + 1) * BLOCK]
                s00, s01, s10, s11 = (turned(cross, r, l) for r in range(2) for l in range(2))
                low0 = jnp.where(wrapped, s01 + s10, s11)
                high0 = jnp.where(wrapped, zero, s00)
                low1 = jnp.where(wrapped, s11, zero)
                high1 = jnp.where(wrapped, s00, s01 + s10)
                low_ref[d + k] = jnp.concatenate([fold(low0), fold(low1)], axis=1)
                high_ref[d + k] = jnp.concatenate([fold(high0), fold(high1)], axis=1)
        parts.append(acc_ref[...].reshape(blocks, GROUP, BLOCK))
        f_ref[g] = (low_ref[...] + high_ref[pl.ds(1, blocks)]).sum(axis=1) * scale
    y_ref[...] = jnp.concatenate(parts, axis=1).astype(BF16)


def conv_forward(x, h):
    blocks = x.shape[0]
    total = blocks * GROUP
    return pl.pallas_call(
        conv_kernel,
        name="conv_forward",
        out_shape=jax.ShapeDtypeStruct(x.shape, BF16),
        scratch_shapes=[
            pltpu.VMEM((h.shape[0], h.shape[1] // HALF + 1, HALF, HALF), BF16),
            pltpu.VMEM((total, LAGS * BLOCK), BF16),
            pltpu.VMEM((total, BLOCK), F32),
        ],
        compiler_params=SCRATCH,
        cost_estimate=pl.CostEstimate(flops=6000000000, bytes_accessed=600000, transcendentals=0),
    )(x, h)


def conv_backward(m, x, h):
    blocks, chans, _ = x.shape
    total = blocks * GROUP
    scale = 1.0 / math.sqrt(GROUP * blocks * BLOCK)
    return pl.pallas_call(
        functools.partial(back_kernel, scale=scale),
        name="conv_backward",
        out_shape=(
            jax.ShapeDtypeStruct(x.shape, BF16),
            jax.ShapeDtypeStruct((chans // GROUP, blocks, BLOCK), F32),
        ),
        scratch_shapes=[
            pltpu.VMEM((h.shape[0], h.shape[1] // HALF + 1, HALF, HALF), BF16),
            pltpu.VMEM((total + total // 2, LAGS * BLOCK), BF16),
            pltpu.VMEM((total, BLOCK), F32),
            pltpu.VMEM((blocks, 8, BLOCK), F32),
            pltpu.VMEM((blocks + 1, 8, BLOCK), F32),
        ],
        compiler_params=SCRATCH,
        cost_estimate=pl.CostEstimate(flops=10000000000, bytes_accessed=1000000, transcendentals=0),
    )(m, x, h)


def whole_columns(at_ref, sign, step, refs):
    own, own_c, side, side_c, own2, own_c2, side2, side_c2 = refs
    first = at_ref[1] == 0
    met = ((at_ref[2] + step) & 1) * 4 + ((at_ref[3] + sign * (step // 2) + 4) & 3)
    apart = at_ref[4] ^ met
    early = (apart & 1) == 0
    place = (apart & 2) + (apart >> 2)

    def pick(a, b):
        return jnp.where(early, a[place], b[place])

    parts = []
    for a, b, c, d in ((own, own2, own_c, own_c2), (side, side2, side_c, side_c2)):
        mine, other = pick(a, b), pick(c, d)
        parts += [jnp.where(first, mine, other), jnp.where(first, other, mine)]
    return jnp.concatenate(parts, axis=1)


def side_columns(side, width):
    return pl.ds(pl.multiple_of(side * width, width), width)


def short_side(i, proj_ref, before_ref, taps_ref):
    now = proj_ref[i].astype(F32)
    before = before_ref[i].astype(F32)
    row = lax.broadcasted_iota(jnp.int32, now.shape, 0)
    total = taps_ref[i, SHORT - 1 : SHORT, :] * now
    for j in range(1, SHORT):
        late = pltpu.roll(now, j, 0)
        for r in range(j):
            late = jnp.where(row == r, before[SHORT - 1 - j + r][None, :], late)
        total = total + taps_ref[i, SHORT - 1 - j : SHORT - j, :] * late
    return total


def grad_mm_kernel(at_ref, proj_ref, before_ref, taps_ref, cot0, cot1, cot2, cot3, *refs):
    *w_refs, out_ref, mixed_ref, sent_ref = refs
    yl = at_ref[0]
    width = cot0.shape[2] // 2
    for step in range(8):
        cot_ref = (cot0, cot1, cot2, cot3)[step // 2]
        e = step % 2
        lhs = jnp.concatenate(
            [cot_ref[e, :, side_columns(yl, width)], cot_ref[e, :, side_columns(1 - yl, width)]],
            axis=1,
        )
        part = lax.dot_general(
            lhs,
            whole_columns(at_ref, -1, step, w_refs),
            (((1,), (1,)), ((), ())),
            preferred_element_type=F32,
        )
        if step == 0:
            out_ref[...] = part
        else:
            out_ref[...] += part
    mixed = (out_ref[...] * short_side(0, proj_ref, before_ref, taps_ref)).astype(BF16)
    mixed_ref[...] = mixed
    sent_ref[...] = mixed.astype(F32).T.astype(BF16)


SCALARS = pl.BlockSpec(memory_space=pltpu.SMEM)
WHOLE = pl.BlockSpec(memory_space=pltpu.VMEM)


def grad_matmul(at, side_args, cots, ws):
    _, tok, rows = side_args[0].shape
    return pl.pallas_call(
        grad_mm_kernel,
        name="grad_matmul",
        out_shape=(
            OUTSIDE((tok, rows), F32),
            OUTSIDE((tok, rows), BF16),
            OUTSIDE((rows, tok), BF16),
        ),
        in_specs=[SCALARS] + [WHOLE] * (len(side_args) + len(cots) + len(ws)),
        out_specs=(WHOLE,) * 3,
        compiler_params=SCRATCH,
        cost_estimate=pl.CostEstimate(flops=4000000000, bytes_accessed=6500000, transcendentals=0),
    )(at, *side_args, *cots, *ws)


def mix_mm_kernel(at_ref, conv_ref, proj_ref, before_ref, taps_ref, skip_ref, grad_ref, *refs):
    *w_refs, out0, out1, out2, out3, query_grad_ref = refs
    yl = at_ref[0]
    conv = conv_ref[...].astype(F32).T
    query, key, value = (short_side(i, proj_ref, before_ref, taps_ref) for i in range(3))
    mixed_in = conv + skip_ref[...] * (key * value).astype(BF16).astype(F32)
    query_grad_ref[...] = grad_ref[...] * mixed_in
    gated = (query * mixed_in).astype(BF16)
    width = out0.shape[2] // 2
    for step in range(8):
        out_ref = (out0, out1, out2, out3)[step // 2]
        e = step % 2
        part = jnp.dot(
            gated, whole_columns(at_ref, 1, step, w_refs), preferred_element_type=F32
        ).astype(BF16)
        out_ref[e, :, side_columns(yl, width)] = part[:, :width]
        out_ref[e, :, side_columns(1 - yl, width)] = part[:, width:]


def mix_matmul(at, conv, side_args, skip, grad, ws):
    tok, rows = grad.shape
    cols = 4 * ws[0].shape[2]
    *parts, query_grad = pl.pallas_call(
        mix_mm_kernel,
        name="mix_matmul",
        out_shape=(OUTSIDE((2, tok, cols), BF16),) * 4 + (OUTSIDE((tok, rows), F32),),
        in_specs=[SCALARS] + [WHOLE] * (3 + len(side_args) + len(ws)),
        out_specs=(WHOLE,) * 5,
        compiler_params=SCRATCH,
        cost_estimate=pl.CostEstimate(flops=4000000000, bytes_accessed=6500000, transcendentals=0),
    )(at, conv, *side_args, skip, grad, *ws)
    return parts, query_grad


def cross_z(shard, by):
    return lax.ppermute(shard, "z", [(i, i ^ by) for i in range(lax.axis_size("z"))])


def shift_x(shard, by):
    count = lax.axis_size("x")
    return lax.ppermute(shard, "x", [(i, (i + by) % count) for i in range(count)])


def pre_kernel(proj_ref, before_ref, taps_ref, sent_ref):
    key, value = (short_side(i, proj_ref, before_ref, taps_ref) for i in (1, 2))
    sent_ref[...] = (key * value).T.astype(BF16)


def carried_columns(side_args):
    _, tok, cols = side_args[0].shape
    return pl.pallas_call(
        pre_kernel,
        name="carried_columns",
        out_shape=OUTSIDE((cols, tok), BF16),
        compiler_params=SCRATCH,
        cost_estimate=pl.CostEstimate(flops=5000000, bytes_accessed=1500000, transcendentals=0),
    )(*side_args)


def final_kernel(
    back_ref, mixed_ref, query_grad_ref, proj_ref, before_ref, taps_ref, skip_ref, out_ref, head_ref, tail_ref
):
    tok = mixed_ref.shape[0]
    row = lax.broadcasted_iota(jnp.int32, mixed_ref.shape, 0)
    carried_grad = back_ref[...].astype(F32).T + skip_ref[...] * mixed_ref[...].astype(F32)
    key, value = (short_side(i, proj_ref, before_ref, taps_ref) for i in (1, 2))
    grads = (query_grad_ref[...], carried_grad * value, carried_grad * key)
    for i, grad in enumerate(grads):
        head_ref[i] = grad[: head_ref.shape[1]]
        total = taps_ref[i, SHORT - 1 : SHORT, :] * grad
        for j in range(1, SHORT):
            early = jnp.where(row < tok - j, pltpu.roll(grad, tok - j, 0), 0.0)
            total = total + taps_ref[i, SHORT - 1 - j : SHORT - j, :] * early
        out_ref[i] = total.astype(BF16)
        tail_ref[i] = total[tok - EDGE :]


def final_short(back, mixed_grad, query_grad, side_args, skip):
    tok, cols = mixed_grad.shape
    return pl.pallas_call(
        final_kernel,
        name="final_short",
        out_shape=(
            jax.ShapeDtypeStruct((3, tok, cols), BF16),
            OUTSIDE((3, 8, cols), F32),
            jax.ShapeDtypeStruct((3, EDGE, cols), F32),
        ),
        compiler_params=SCRATCH,
        cost_estimate=pl.CostEstimate(flops=5000000, bytes_accessed=3500000, transcendentals=0),
    )(back, mixed_grad, query_grad, *side_args, skip)


def edge_kernel(tail_ref, after_ref, taps_ref, whole_ref, out_ref):
    row = lax.broadcasted_iota(jnp.int32, tail_ref.shape[1:], 0)
    for i in range(3):
        after = after_ref[i]
        total = tail_ref[i]
        for s in range(SHORT - 1):
            missing = sum(
                taps_ref[i, SHORT - 2 - s - r : SHORT - 1 - s - r, :] * after[r : r + 1]
                for r in range(SHORT - 1 - s)
            )
            total = total + jnp.where(row == EDGE - 1 - s, 1.0, 0.0) * missing
        out_ref[i] = total.astype(BF16)


def edge_rows(tail, after, taps, whole):
    _, tok, cols = whole.shape
    return pl.pallas_call(
        edge_kernel,
        name="edge_rows",
        out_shape=jax.ShapeDtypeStruct(whole.shape, BF16),
        grid=(1,),
        in_specs=[
            pl.BlockSpec(tail.shape, lambda i: (0, 0, 0)),
            pl.BlockSpec(after.shape, lambda i: (0, 0, 0)),
            pl.BlockSpec(taps.shape, lambda i: (0, 0, 0)),
            pl.BlockSpec(memory_space=pl.ANY),
        ],
        out_specs=pl.BlockSpec((3, EDGE, cols), lambda i: (0, tok // EDGE - 1, 0)),
        input_output_aliases={3: 0},
        compiler_params=SCRATCH,
        cost_estimate=pl.CostEstimate(flops=500000, bytes_accessed=200000, transcendentals=0),
    )(tail, after, taps, whole)


def channel_major(sent):
    count = lax.axis_size(SEQ)
    sent = sent.reshape(count, sent.shape[0] // count, sent.shape[1])
    return lax.all_to_all(sent, SEQ, split_axis=0, concat_axis=0, tiled=True)


def token_major(block):
    got = lax.all_to_all(block, SEQ, split_axis=0, concat_axis=0, tiled=True)
    return got.reshape(got.shape[0] * got.shape[1], got.shape[2])


def on_device(projected, short_weight, filters, skip, out_weight, cotangent):
    tok_rows, _ = cotangent.shape
    groups_dev, seq_length = filters.shape
    rim = SHORT - 1
    wide = lax.axis_size("x")
    yl, core = lax.axis_index("yl"), lax.axis_index("core")
    yh, x, z = lax.axis_index("yh"), lax.axis_index("x"), lax.axis_index("z")

    at = jnp.stack([yl, core, yh, x, z]).astype(jnp.int32)
    before = from_behind(projected[tok_rows - rim :], 1)
    cot_pair = jnp.stack([cotangent, swap(cotangent, "yh")])
    cots = [cot_pair] + [shift_x(cot_pair, k) for k in range(1, wide)]
    w_pair = jnp.stack([out_weight, cross_z(out_weight, 4)])
    w_own = jnp.concatenate([w_pair, cross_z(w_pair, 2)])
    w_own2 = cross_z(w_own, 1)
    w_side = swap(w_own, "yl")
    w_side2 = swap(w_own2, "yl")
    w_own_c = swap(w_own, "core")
    w_side_c = swap(w_side, "core")
    w_own_c2 = swap(w_own2, "core")
    w_side_c2 = swap(w_side2, "core")
    ws = (w_own, w_own_c, w_side, w_side_c, w_own2, w_own_c2, w_side2, w_side_c2)

    side_args = (projected.transpose(1, 0, 2), before.transpose(1, 0, 2), short_weight)
    carried_sent = carried_columns(side_args)
    carried_seq = channel_major(carried_sent)
    conv_seq = conv_forward(carried_seq, filters)
    conv = token_major(conv_seq)

    gated_grad, mixed_grad, grad_sent = grad_matmul(at, side_args, cots, ws)
    grad_seq = channel_major(grad_sent)

    parts, query_grad = mix_matmul(at, conv, side_args, skip[None, :], gated_grad, ws)
    shares = [parts[0]] + [shift_x(parts[k], k) for k in range(1, wide)]
    theirs = sum(p[1].astype(F32) for p in shares).astype(BF16)
    got = swap(theirs, "yh")
    mixed = (sum(p[0].astype(F32) for p in shares) + got.astype(F32)).astype(BF16)

    back_seq, filter_grad = conv_backward(grad_seq, carried_seq, filters)
    back = token_major(back_seq)
    whole, head, tail = final_short(back, mixed_grad, query_grad, side_args, skip[None, :])
    after = from_behind(head, -1)
    projected_grad = edge_rows(tail, after, short_weight, whole)
    return (
        mixed,
        projected_grad.transpose(1, 0, 2),
        filter_grad.reshape(groups_dev, seq_length),
    )


def solution(mesh):
    fine = Mesh(mesh.devices.reshape(8, 2, 2, 2, 4), ("z", "yl", "core", "yh", "x"))
    placed = (
        P(SEQ, None, CHAN),
        P(None, None, CHAN),
        P(CHAN + SEQ, None),
        P(CHAN),
        P(CHAN, SEQ),
        P(SEQ, CHAN),
    )
    return jax.shard_map(
        on_device,
        mesh=fine,
        in_specs=placed,
        out_specs=(P(SEQ, CHAN), P(SEQ, None, CHAN), P(CHAN + SEQ, None)),
        check_vma=False,
    )
```

```python
import functools
import math

import jax
import jax.numpy as jnp
from jax import lax
from jax.experimental import pallas as pl
from jax.experimental.pallas import tpu as pltpu
from jax.sharding import Mesh, PartitionSpec as P


GROUP = 8
SHORT = 3
BLOCK = 256
HALF = 128
LAGS = 4
SCRATCH = pltpu.CompilerParams(vmem_limit_bytes=24 << 20)
BUILD_UNROLL = 16
EDGE = 16
OUTSIDE = pltpu.HBM

SEQ = ("z", "yl", "core")
CHAN = ("yh", "x")
F32 = jnp.float32
BF16 = jnp.bfloat16


def from_behind(shard, by):
    count = lax.axis_size(SEQ)
    pairs = [(i, i + by) for i in range(count) if 0 <= i + by < count]
    return lax.ppermute(shard, SEQ, pairs)


def swap(shard, axis):
    return lax.ppermute(shard, axis, [(0, 1), (1, 0)])


def skew_masks():
    rows = lax.broadcasted_iota(jnp.int32, (HALF, HALF), 0)
    lanes = lax.broadcasted_iota(jnp.int32, (HALF, HALF), 1)
    return rows, lanes


def build_tiles(h_ref, tile_ref):
    groups, count = tile_ref.shape[0], tile_ref.shape[1] - 1
    rows, lanes = skew_masks()
    inside = lanes >= rows
    zero = jnp.zeros((HALF, HALF), F32)
    for g in range(groups):
        tile_ref[g, 0] = zero.astype(BF16)

    def step(j, before):
        turns = []
        for g in range(groups):
            row = h_ref[g : g + 1, pl.ds(pl.multiple_of(j * HALF, HALF), HALF)]
            turned = pltpu.roll(jnp.broadcast_to(row, (HALF, HALF)), 0, 1, stride=1, stride_axis=0)
            tile_ref[g, j + 1] = jnp.where(inside, turned, before[g]).astype(BF16)
            turns.append(turned)
        return tuple(turns)

    lax.fori_loop(0, count, step, (zero,) * groups, unroll=BUILD_UNROLL)


def toeplitz_block(tile_ref, g, d):
    same = tile_ref[g, 2 * d + 1]
    upper = jnp.concatenate([same, tile_ref[g, 2 * d + 2]], axis=1)
    lower = jnp.concatenate([tile_ref[g, 2 * d], same], axis=1)
    return jnp.concatenate([upper, lower], axis=0)


def group_rows(ref, g):
    part = ref[...].astype(F32)[:, g * GROUP : (g + 1) * GROUP, :]
    return part.reshape(part.shape[0] * GROUP, BLOCK)


def conv_kernel(x_ref, h_ref, y_ref, tile_ref, wide_ref, acc_ref):
    blocks, chans, _ = x_ref.shape
    total = blocks * GROUP
    parts = []
    build_tiles(h_ref, tile_ref)
    for g in range(chans // GROUP):
        signal = group_rows(x_ref, g)
        for k in range(LAGS):
            late = signal
            if k > 0:
                late = jnp.concatenate(
                    [jnp.zeros((k * GROUP, BLOCK), F32), signal[: total - k * GROUP]], axis=0
                )
            wide_ref[:, k * BLOCK : (k + 1) * BLOCK] = late.astype(BF16)
        for d in range(0, blocks, LAGS):
            rows = total - d * GROUP
            weights = jnp.concatenate(
                [toeplitz_block(tile_ref, g, d + k) for k in range(LAGS)], axis=0
            )
            part = jnp.dot(wide_ref[:rows, :], weights, preferred_element_type=F32)
            if d == 0:
                acc_ref[...] = part
            else:
                acc_ref[d * GROUP :, :] += part
        parts.append(acc_ref[...].reshape(blocks, GROUP, BLOCK))
    y_ref[...] = jnp.concatenate(parts, axis=1).astype(BF16)


def back_kernel(m_ref, x_ref, h_ref, y_ref, f_ref, tile_ref, wide_ref, acc_ref, low_ref, high_ref, *, scale):
    blocks, chans, _ = x_ref.shape
    total = blocks * GROUP
    rows_i, lanes_i = skew_masks()
    wrapped = lanes_i <= rows_i
    flip = (
        lax.broadcasted_iota(jnp.int32, (BLOCK, BLOCK), 0)
        + lax.broadcasted_iota(jnp.int32, (BLOCK, BLOCK), 1)
        == BLOCK - 1
    )
    flip = jnp.where(flip, 1.0, 0.0).astype(BF16)
    zero = jnp.zeros((HALF, HALF), F32)
    build_tiles(h_ref, tile_ref)
    parts = []

    def fold(v):
        return v.reshape(HALF // 8, 8, HALF).sum(axis=0)

    def turned(cross, r, l):
        return pltpu.roll(
            cross[r * HALF : (r + 1) * HALF, l * HALF : (l + 1) * HALF], 1, 1, stride=1, stride_axis=0
        )

    for g in range(chans // GROUP):
        grad = group_rows(m_ref, g)
        wide_ref[total:, :] = jnp.zeros((wide_ref.shape[0] - total, LAGS * BLOCK), BF16)
        for k in range(LAGS):
            early = grad
            if k > 0:
                early = jnp.concatenate(
                    [grad[k * GROUP :], jnp.zeros((k * GROUP, BLOCK), F32)], axis=0
                )
            wide_ref[:total, k * BLOCK : (k + 1) * BLOCK] = early.astype(BF16)
        signal = group_rows(x_ref, g).astype(BF16)
        flipped = lax.dot_general(
            flip, signal, (((1,), (1,)), ((), ())), preferred_element_type=F32
        ).astype(BF16)
        high_ref[blocks] = jnp.zeros((8, BLOCK), F32)
        for d in range(0, blocks, LAGS):
            rows = total - d * GROUP
            weights = jnp.concatenate(
                [toeplitz_block(tile_ref, g, d + k) for k in range(LAGS)], axis=1
            )
            part = lax.dot_general(
                wide_ref[d * GROUP : total, :],
                weights,
                (((1,), (1,)), ((), ())),
                preferred_element_type=F32,
            )
            if d == 0:
                acc_ref[...] = part
            else:
                acc_ref[:rows, :] += part
            depth = total if 2 * d < blocks else total // 2
            cross_all = jnp.dot(
                flipped[:, :depth],
                wide_ref[d * GROUP : d * GROUP + depth, :],
                preferred_element_type=F32,
            )
            for k in range(LAGS):
                cross = cross_all[:, k * BLOCK : (k + 1) * BLOCK]
                s00, s01, s10, s11 = (turned(cross, r, l) for r in range(2) for l in range(2))
                low0 = jnp.where(wrapped, s01 + s10, s11)
                high0 = jnp.where(wrapped, zero, s00)
                low1 = jnp.where(wrapped, s11, zero)
                high1 = jnp.where(wrapped, s00, s01 + s10)
                low_ref[d + k] = jnp.concatenate([fold(low0), fold(low1)], axis=1)
                high_ref[d + k] = jnp.concatenate([fold(high0), fold(high1)], axis=1)
        parts.append(acc_ref[...].reshape(blocks, GROUP, BLOCK))
        f_ref[g] = (low_ref[...] + high_ref[pl.ds(1, blocks)]).sum(axis=1) * scale
    y_ref[...] = jnp.concatenate(parts, axis=1).astype(BF16)


def conv_forward(x, h):
    blocks = x.shape[0]
    total = blocks * GROUP
    return pl.pallas_call(
        conv_kernel,
        name="conv_forward",
        out_shape=jax.ShapeDtypeStruct(x.shape, BF16),
        scratch_shapes=[
            pltpu.VMEM((h.shape[0], h.shape[1] // HALF + 1, HALF, HALF), BF16),
            pltpu.VMEM((total, LAGS * BLOCK), BF16),
            pltpu.VMEM((total, BLOCK), F32),
        ],
        compiler_params=SCRATCH,
        cost_estimate=pl.CostEstimate(flops=6000000000, bytes_accessed=600000, transcendentals=0),
    )(x, h)


def conv_backward(m, x, h):
    blocks, chans, _ = x.shape
    total = blocks * GROUP
    scale = 1.0 / math.sqrt(GROUP * blocks * BLOCK)
    return pl.pallas_call(
        functools.partial(back_kernel, scale=scale),
        name="conv_backward",
        out_shape=(
            jax.ShapeDtypeStruct(x.shape, BF16),
            jax.ShapeDtypeStruct((chans // GROUP, blocks, BLOCK), F32),
        ),
        scratch_shapes=[
            pltpu.VMEM((h.shape[0], h.shape[1] // HALF + 1, HALF, HALF), BF16),
            pltpu.VMEM((total + total // 2, LAGS * BLOCK), BF16),
            pltpu.VMEM((total, BLOCK), F32),
            pltpu.VMEM((blocks, 8, BLOCK), F32),
            pltpu.VMEM((blocks + 1, 8, BLOCK), F32),
        ],
        compiler_params=SCRATCH,
        cost_estimate=pl.CostEstimate(flops=10000000000, bytes_accessed=1000000, transcendentals=0),
    )(m, x, h)


def met_places(at_ref, sign):
    z = at_ref[4]
    for first in (z, (z + 1) & 7, (z + 7) & 7, z ^ 2):
        for chan in (first, first ^ 4):
            yield (sign * ((chan & 3) - at_ref[3])) & 3, (chan >> 2) ^ at_ref[2]


def whole_columns(at_ref, place, refs):
    first = at_ref[1] == 0
    own, own_c, side, side_c = (ref[place % 2] for ref in refs[place // 2 * 4 : place // 2 * 4 + 4])
    parts = []
    for mine, other in ((own, own_c), (side, side_c)):
        parts += [jnp.where(first, mine, other), jnp.where(first, other, mine)]
    return jnp.concatenate(parts, axis=1)


def side_columns(side, width):
    return pl.ds(pl.multiple_of(side * width, width), width)


def short_side(i, proj_ref, before_ref, taps_ref):
    now = proj_ref[i].astype(F32)
    before = before_ref[i].astype(F32)
    row = lax.broadcasted_iota(jnp.int32, now.shape, 0)
    total = taps_ref[i, SHORT - 1 : SHORT, :] * now
    for j in range(1, SHORT):
        late = pltpu.roll(now, j, 0)
        for r in range(j):
            late = jnp.where(row == r, before[SHORT - 1 - j + r][None, :], late)
        total = total + taps_ref[i, SHORT - 1 - j : SHORT - j, :] * late
    return total


def grad_mm_kernel(at_ref, proj_ref, before_ref, taps_ref, cot0, cot1, cot2, cot3, *refs):
    *w_refs, out_ref, mixed_ref, sent_ref = refs
    yl = at_ref[0]
    width = cot0.shape[2] // 2
    for step, (k, e) in enumerate(met_places(at_ref, -1)):
        halves = []
        for at in (yl, 1 - yl):
            c0, c1, c2, c3 = (
                cot_ref[e, :, side_columns(at, width)] for cot_ref in (cot0, cot1, cot2, cot3)
            )
            halves.append(jnp.where(k < 2, jnp.where(k == 0, c0, c1), jnp.where(k == 2, c2, c3)))
        lhs = jnp.concatenate(halves, axis=1)
        part = lax.dot_general(
            lhs,
            whole_columns(at_ref, step, w_refs),
            (((1,), (1,)), ((), ())),
            preferred_element_type=F32,
        )
        if step == 0:
            out_ref[...] = part
        else:
            out_ref[...] += part
    mixed = (out_ref[...] * short_side(0, proj_ref, before_ref, taps_ref)).astype(BF16)
    mixed_ref[...] = mixed
    sent_ref[...] = mixed.astype(F32).T.astype(BF16)


SCALARS = pl.BlockSpec(memory_space=pltpu.SMEM)
WHOLE = pl.BlockSpec(memory_space=pltpu.VMEM)


def grad_matmul(at, side_args, cots, ws):
    _, tok, rows = side_args[0].shape
    return pl.pallas_call(
        grad_mm_kernel,
        name="grad_matmul",
        out_shape=(
            OUTSIDE((tok, rows), F32),
            OUTSIDE((tok, rows), BF16),
            OUTSIDE((rows, tok), BF16),
        ),
        in_specs=[SCALARS] + [WHOLE] * (len(side_args) + len(cots) + len(ws)),
        out_specs=(WHOLE,) * 3,
        compiler_params=SCRATCH,
        cost_estimate=pl.CostEstimate(flops=4000000000, bytes_accessed=6500000, transcendentals=0),
    )(at, *side_args, *cots, *ws)


def mix_mm_kernel(at_ref, conv_ref, proj_ref, before_ref, taps_ref, skip_ref, grad_ref, *refs):
    *w_refs, out0, out1, out2, out3, query_grad_ref = refs
    yl = at_ref[0]
    conv = conv_ref[...].astype(F32).T
    query, key, value = (short_side(i, proj_ref, before_ref, taps_ref) for i in range(3))
    mixed_in = conv + skip_ref[...] * (key * value).astype(BF16).astype(F32)
    query_grad_ref[...] = grad_ref[...] * mixed_in
    gated = (query * mixed_in).astype(BF16)
    width = out0.shape[2] // 2
    for step, (k, e) in enumerate(met_places(at_ref, 1)):
        part = jnp.dot(
            gated, whole_columns(at_ref, step, w_refs), preferred_element_type=F32
        ).astype(BF16)
        for turn, out_ref in enumerate((out0, out1, out2, out3)):

            @pl.when(k == turn)
            def _(out_ref=out_ref, part=part, e=e):
                out_ref[e, :, side_columns(yl, width)] = part[:, :width]
                out_ref[e, :, side_columns(1 - yl, width)] = part[:, width:]


def mix_matmul(at, conv, side_args, skip, grad, ws):
    tok, rows = grad.shape
    cols = 4 * ws[0].shape[-1]
    *parts, query_grad = pl.pallas_call(
        mix_mm_kernel,
        name="mix_matmul",
        out_shape=(OUTSIDE((2, tok, cols), BF16),) * 4 + (OUTSIDE((tok, rows), F32),),
        in_specs=[SCALARS] + [WHOLE] * (3 + len(side_args) + len(ws)),
        out_specs=(WHOLE,) * 5,
        compiler_params=SCRATCH,
        cost_estimate=pl.CostEstimate(flops=4000000000, bytes_accessed=6500000, transcendentals=0),
    )(at, conv, *side_args, skip, grad, *ws)
    return parts, query_grad


def shift_z(shard, by):
    count = lax.axis_size("z")
    return lax.ppermute(shard, "z", [(i, (i + by) % count) for i in range(count)])


def cross_z(shard, by):
    return lax.ppermute(shard, "z", [(i, i ^ by) for i in range(lax.axis_size("z"))])


def shift_x(shard, by):
    count = lax.axis_size("x")
    return lax.ppermute(shard, "x", [(i, (i + by) % count) for i in range(count)])


def pre_kernel(proj_ref, before_ref, taps_ref, sent_ref):
    key, value = (short_side(i, proj_ref, before_ref, taps_ref) for i in (1, 2))
    sent_ref[...] = (key * value).T.astype(BF16)


def carried_columns(side_args):
    _, tok, cols = side_args[0].shape
    return pl.pallas_call(
        pre_kernel,
        name="carried_columns",
        out_shape=OUTSIDE((cols, tok), BF16),
        compiler_params=SCRATCH,
        cost_estimate=pl.CostEstimate(flops=5000000, bytes_accessed=1500000, transcendentals=0),
    )(*side_args)


def final_kernel(
    back_ref, mixed_ref, query_grad_ref, proj_ref, before_ref, taps_ref, skip_ref, out_ref, head_ref, tail_ref
):
    tok = mixed_ref.shape[0]
    row = lax.broadcasted_iota(jnp.int32, mixed_ref.shape, 0)
    carried_grad = back_ref[...].astype(F32).T + skip_ref[...] * mixed_ref[...].astype(F32)
    key, value = (short_side(i, proj_ref, before_ref, taps_ref) for i in (1, 2))
    grads = (query_grad_ref[...], carried_grad * value, carried_grad * key)
    for i, grad in enumerate(grads):
        head_ref[i] = grad[: head_ref.shape[1]]
        total = taps_ref[i, SHORT - 1 : SHORT, :] * grad
        for j in range(1, SHORT):
            early = jnp.where(row < tok - j, pltpu.roll(grad, tok - j, 0), 0.0)
            total = total + taps_ref[i, SHORT - 1 - j : SHORT - j, :] * early
        out_ref[i] = total.astype(BF16)
        tail_ref[i] = total[tok - EDGE :]


def final_short(back, mixed_grad, query_grad, side_args, skip):
    tok, cols = mixed_grad.shape
    return pl.pallas_call(
        final_kernel,
        name="final_short",
        out_shape=(
            jax.ShapeDtypeStruct((3, tok, cols), BF16),
            OUTSIDE((3, 8, cols), F32),
            jax.ShapeDtypeStruct((3, EDGE, cols), F32),
        ),
        compiler_params=SCRATCH,
        cost_estimate=pl.CostEstimate(flops=5000000, bytes_accessed=3500000, transcendentals=0),
    )(back, mixed_grad, query_grad, *side_args, skip)


def edge_kernel(tail_ref, after_ref, taps_ref, whole_ref, out_ref):
    row = lax.broadcasted_iota(jnp.int32, tail_ref.shape[1:], 0)
    for i in range(3):
        after = after_ref[i]
        total = tail_ref[i]
        for s in range(SHORT - 1):
            missing = sum(
                taps_ref[i, SHORT - 2 - s - r : SHORT - 1 - s - r, :] * after[r : r + 1]
                for r in range(SHORT - 1 - s)
            )
            total = total + jnp.where(row == EDGE - 1 - s, 1.0, 0.0) * missing
        out_ref[i] = total.astype(BF16)


def edge_rows(tail, after, taps, whole):
    _, tok, cols = whole.shape
    return pl.pallas_call(
        edge_kernel,
        name="edge_rows",
        out_shape=jax.ShapeDtypeStruct(whole.shape, BF16),
        grid=(1,),
        in_specs=[
            pl.BlockSpec(tail.shape, lambda i: (0, 0, 0)),
            pl.BlockSpec(after.shape, lambda i: (0, 0, 0)),
            pl.BlockSpec(taps.shape, lambda i: (0, 0, 0)),
            pl.BlockSpec(memory_space=pl.ANY),
        ],
        out_specs=pl.BlockSpec((3, EDGE, cols), lambda i: (0, tok // EDGE - 1, 0)),
        input_output_aliases={3: 0},
        compiler_params=SCRATCH,
        cost_estimate=pl.CostEstimate(flops=500000, bytes_accessed=200000, transcendentals=0),
    )(tail, after, taps, whole)


def channel_major(sent):
    count = lax.axis_size(SEQ)
    sent = sent.reshape(count, sent.shape[0] // count, sent.shape[1])
    return lax.all_to_all(sent, SEQ, split_axis=0, concat_axis=0, tiled=True)


def token_major(block):
    got = lax.all_to_all(block, SEQ, split_axis=0, concat_axis=0, tiled=True)
    return got.reshape(got.shape[0] * got.shape[1], got.shape[2])


def on_device(projected, short_weight, filters, skip, out_weight, cotangent):
    tok_rows, _ = cotangent.shape
    groups_dev, seq_length = filters.shape
    rim = SHORT - 1
    wide, deep = lax.axis_size("x"), lax.axis_size("z")
    yl, core = lax.axis_index("yl"), lax.axis_index("core")
    yh, x, z = lax.axis_index("yh"), lax.axis_index("x"), lax.axis_index("z")

    at = jnp.stack([yl, core, yh, x, z]).astype(jnp.int32)
    before = from_behind(projected[tok_rows - rim :], 1)
    cot_pair = jnp.stack([cotangent, swap(cotangent, "yh")])
    cots = [cot_pair] + [shift_x(cot_pair, k) for k in range(1, wide)]
    w_pair = jnp.stack([out_weight, cross_z(out_weight, 4)])
    pairs = [shift_z(w_pair, deep - 1), shift_z(w_pair, 1), cross_z(w_pair, 2)]
    sides = [swap(w_pair, "yl")]
    sides += [swap(p, "yl") for p in pairs]
    pairs = [w_pair] + pairs
    pairs_c = [swap(p, "core") for p in pairs]
    sides_c = [swap(p, "core") for p in sides]
    ws = tuple(w for group in zip(pairs, pairs_c, sides, sides_c) for w in group)

    side_args = (projected.transpose(1, 0, 2), before.transpose(1, 0, 2), short_weight)
    carried_sent = carried_columns(side_args)
    carried_seq = channel_major(carried_sent)
    conv_seq = conv_forward(carried_seq, filters)
    conv = token_major(conv_seq)

    gated_grad, mixed_grad, grad_sent = grad_matmul(at, side_args, cots, ws)
    grad_seq = channel_major(grad_sent)

    parts, query_grad = mix_matmul(at, conv, side_args, skip[None, :], gated_grad, ws)
    shares = [parts[0]] + [shift_x(parts[k], k) for k in range(1, wide)]
    theirs = sum(p[1].astype(F32) for p in shares).astype(BF16)
    got = swap(theirs, "yh")
    mixed = (sum(p[0].astype(F32) for p in shares) + got.astype(F32)).astype(BF16)

    back_seq, filter_grad = conv_backward(grad_seq, carried_seq, filters)
    back = token_major(back_seq)
    whole, head, tail = final_short(back, mixed_grad, query_grad, side_args, skip[None, :])
    after = from_behind(head, -1)
    projected_grad = edge_rows(tail, after, short_weight, whole)
    return (
        mixed,
        projected_grad.transpose(1, 0, 2),
        filter_grad.reshape(groups_dev, seq_length),
    )


def solution(mesh):
    fine = Mesh(mesh.devices.reshape(8, 2, 2, 2, 4), ("z", "yl", "core", "yh", "x"))
    placed = (
        P(SEQ, None, CHAN),
        P(None, None, CHAN),
        P(CHAN + SEQ, None),
        P(CHAN),
        P(CHAN, SEQ),
        P(SEQ, CHAN),
    )
    return jax.shard_map(
        on_device,
        mesh=fine,
        in_specs=placed,
        out_specs=(P(SEQ, CHAN), P(SEQ, None, CHAN), P(CHAN + SEQ, None)),
        check_vma=False,
    )
```

```python
import functools
import math

import jax
import jax.numpy as jnp
from jax import lax
from jax.experimental import pallas as pl
from jax.experimental.pallas import tpu as pltpu
from jax.sharding import Mesh, PartitionSpec as P


GROUP = 8
SHORT = 3
BLOCK = 256
HALF = 128
LAGS = 4
SCRATCH = pltpu.CompilerParams(vmem_limit_bytes=24 << 20)
BUILD_UNROLL = 16
EDGE = 16
OUTSIDE = pltpu.HBM

SEQ = ("z", "yl", "core")
CHAN = ("yh", "x")
F32 = jnp.float32
BF16 = jnp.bfloat16


def from_behind(shard, by):
    count = lax.axis_size(SEQ)
    pairs = [(i, i + by) for i in range(count) if 0 <= i + by < count]
    return lax.ppermute(shard, SEQ, pairs)


def swap(shard, axis):
    return lax.ppermute(shard, axis, [(0, 1), (1, 0)])


def skew_masks():
    rows = lax.broadcasted_iota(jnp.int32, (HALF, HALF), 0)
    lanes = lax.broadcasted_iota(jnp.int32, (HALF, HALF), 1)
    return rows, lanes


def build_tiles(h_ref, tile_ref):
    groups, count = tile_ref.shape[0], tile_ref.shape[1] - 1
    rows, lanes = skew_masks()
    inside = lanes >= rows
    zero = jnp.zeros((HALF, HALF), F32)
    for g in range(groups):
        tile_ref[g, 0] = zero.astype(BF16)

    def step(j, before):
        turns = []
        for g in range(groups):
            row = h_ref[g : g + 1, pl.ds(pl.multiple_of(j * HALF, HALF), HALF)]
            turned = pltpu.roll(jnp.broadcast_to(row, (HALF, HALF)), 0, 1, stride=1, stride_axis=0)
            tile_ref[g, j + 1] = jnp.where(inside, turned, before[g]).astype(BF16)
            turns.append(turned)
        return tuple(turns)

    lax.fori_loop(0, count, step, (zero,) * groups, unroll=BUILD_UNROLL)


def toeplitz_block(tile_ref, g, d):
    same = tile_ref[g, 2 * d + 1]
    upper = jnp.concatenate([same, tile_ref[g, 2 * d + 2]], axis=1)
    lower = jnp.concatenate([tile_ref[g, 2 * d], same], axis=1)
    return jnp.concatenate([upper, lower], axis=0)


def group_rows(ref, g):
    part = ref[...].astype(F32)[:, g * GROUP : (g + 1) * GROUP, :]
    return part.reshape(part.shape[0] * GROUP, BLOCK)


def conv_kernel(x_ref, h_ref, y_ref, tile_ref, wide_ref, acc_ref):
    blocks, chans, _ = x_ref.shape
    total = blocks * GROUP
    parts = []
    build_tiles(h_ref, tile_ref)
    for g in range(chans // GROUP):
        signal = group_rows(x_ref, g)
        for k in range(LAGS):
            late = signal
            if k > 0:
                late = jnp.concatenate(
                    [jnp.zeros((k * GROUP, BLOCK), F32), signal[: total - k * GROUP]], axis=0
                )
            wide_ref[:, k * BLOCK : (k + 1) * BLOCK] = late.astype(BF16)
        for d in range(0, blocks, LAGS):
            rows = total - d * GROUP
            weights = jnp.concatenate(
                [toeplitz_block(tile_ref, g, d + k) for k in range(LAGS)], axis=0
            )
            part = jnp.dot(wide_ref[:rows, :], weights, preferred_element_type=F32)
            if d == 0:
                acc_ref[...] = part
            else:
                acc_ref[d * GROUP :, :] += part
        parts.append(acc_ref[...].reshape(blocks, GROUP, BLOCK))
    y_ref[...] = jnp.concatenate(parts, axis=1).astype(BF16)


def back_kernel(m_ref, x_ref, h_ref, y_ref, f_ref, tile_ref, wide_ref, acc_ref, low_ref, high_ref, *, scale):
    blocks, chans, _ = x_ref.shape
    total = blocks * GROUP
    rows_i, lanes_i = skew_masks()
    wrapped = lanes_i <= rows_i
    flip = (
        lax.broadcasted_iota(jnp.int32, (BLOCK, BLOCK), 0)
        + lax.broadcasted_iota(jnp.int32, (BLOCK, BLOCK), 1)
        == BLOCK - 1
    )
    flip = jnp.where(flip, 1.0, 0.0).astype(BF16)
    zero = jnp.zeros((HALF, HALF), F32)
    build_tiles(h_ref, tile_ref)
    parts = []

    def fold(v):
        return v.reshape(HALF // 8, 8, HALF).sum(axis=0)

    def turned(cross, r, l):
        return pltpu.roll(
            cross[r * HALF : (r + 1) * HALF, l * HALF : (l + 1) * HALF], 1, 1, stride=1, stride_axis=0
        )

    for g in range(chans // GROUP):
        grad = group_rows(m_ref, g)
        wide_ref[total:, :] = jnp.zeros((wide_ref.shape[0] - total, LAGS * BLOCK), BF16)
        for k in range(LAGS):
            early = grad
            if k > 0:
                early = jnp.concatenate(
                    [grad[k * GROUP :], jnp.zeros((k * GROUP, BLOCK), F32)], axis=0
                )
            wide_ref[:total, k * BLOCK : (k + 1) * BLOCK] = early.astype(BF16)
        signal = group_rows(x_ref, g).astype(BF16)
        flipped = lax.dot_general(
            flip, signal, (((1,), (1,)), ((), ())), preferred_element_type=F32
        ).astype(BF16)
        high_ref[blocks] = jnp.zeros((8, BLOCK), F32)
        for d in range(0, blocks, LAGS):
            rows = total - d * GROUP
            weights = jnp.concatenate(
                [toeplitz_block(tile_ref, g, d + k) for k in range(LAGS)], axis=1
            )
            part = lax.dot_general(
                wide_ref[d * GROUP : total, :],
                weights,
                (((1,), (1,)), ((), ())),
                preferred_element_type=F32,
            )
            if d == 0:
                acc_ref[...] = part
            else:
                acc_ref[:rows, :] += part
            depth = total if 2 * d < blocks else total // 2
            cross_all = jnp.dot(
                flipped[:, :depth],
                wide_ref[d * GROUP : d * GROUP + depth, :],
                preferred_element_type=F32,
            )
            for k in range(LAGS):
                cross = cross_all[:, k * BLOCK : (k + 1) * BLOCK]
                s00, s01, s10, s11 = (turned(cross, r, l) for r in range(2) for l in range(2))
                low0 = jnp.where(wrapped, s01 + s10, s11)
                high0 = jnp.where(wrapped, zero, s00)
                low1 = jnp.where(wrapped, s11, zero)
                high1 = jnp.where(wrapped, s00, s01 + s10)
                low_ref[d + k] = jnp.concatenate([fold(low0), fold(low1)], axis=1)
                high_ref[d + k] = jnp.concatenate([fold(high0), fold(high1)], axis=1)
        parts.append(acc_ref[...].reshape(blocks, GROUP, BLOCK))
        f_ref[g] = (low_ref[...] + high_ref[pl.ds(1, blocks)]).sum(axis=1) * scale
    y_ref[...] = jnp.concatenate(parts, axis=1).astype(BF16)


def conv_forward(x, h):
    blocks = x.shape[0]
    total = blocks * GROUP
    return pl.pallas_call(
        conv_kernel,
        name="conv_forward",
        out_shape=jax.ShapeDtypeStruct(x.shape, BF16),
        scratch_shapes=[
            pltpu.VMEM((h.shape[0], h.shape[1] // HALF + 1, HALF, HALF), BF16),
            pltpu.VMEM((total, LAGS * BLOCK), BF16),
            pltpu.VMEM((total, BLOCK), F32),
        ],
        compiler_params=SCRATCH,
        cost_estimate=pl.CostEstimate(flops=6000000000, bytes_accessed=600000, transcendentals=0),
    )(x, h)


def conv_backward(m, x, h):
    blocks, chans, _ = x.shape
    total = blocks * GROUP
    scale = 1.0 / math.sqrt(GROUP * blocks * BLOCK)
    return pl.pallas_call(
        functools.partial(back_kernel, scale=scale),
        name="conv_backward",
        out_shape=(
            jax.ShapeDtypeStruct(x.shape, BF16),
            jax.ShapeDtypeStruct((chans // GROUP, blocks, BLOCK), F32),
        ),
        scratch_shapes=[
            pltpu.VMEM((h.shape[0], h.shape[1] // HALF + 1, HALF, HALF), BF16),
            pltpu.VMEM((total + total // 2, LAGS * BLOCK), BF16),
            pltpu.VMEM((total, BLOCK), F32),
            pltpu.VMEM((blocks, 8, BLOCK), F32),
            pltpu.VMEM((blocks + 1, 8, BLOCK), F32),
        ],
        compiler_params=SCRATCH,
        cost_estimate=pl.CostEstimate(flops=10000000000, bytes_accessed=1000000, transcendentals=0),
    )(m, x, h)


def met_places(at_ref, sign):
    z = at_ref[4]
    for first in (z, (z + 1) & 7, (z + 7) & 7, z ^ 2):
        for chan in (first, first ^ 4):
            yield (sign * ((chan & 3) - at_ref[3])) & 3, (chan >> 2) ^ at_ref[2]


def outside(array):
    return pltpu.with_memory_space_constraint(array, pltpu.HBM)


def piece_copy(source, target, sems, n):
    return pltpu.make_async_copy(source, target, sems.at[n])


def weight_copies(refs, buffer_ref, sems):
    return [piece_copy(ref, buffer_ref.at[n], sems, n) for n, ref in enumerate(refs)]


def whole_columns(at_ref, place, buffer_ref):
    first = at_ref[1] == 0
    own, own_c, side, side_c = (buffer_ref[place // 2 * 4 + n, place % 2] for n in range(4))
    parts = []
    for mine, other in ((own, own_c), (side, side_c)):
        parts += [jnp.where(first, mine, other), jnp.where(first, other, mine)]
    return jnp.concatenate(parts, axis=1)


def side_columns(side, width):
    return pl.ds(pl.multiple_of(side * width, width), width)


def short_side(i, proj_ref, before_ref, taps_ref):
    now = proj_ref[i].astype(F32)
    before = before_ref[i].astype(F32)
    row = lax.broadcasted_iota(jnp.int32, now.shape, 0)
    total = taps_ref[i, SHORT - 1 : SHORT, :] * now
    for j in range(1, SHORT):
        late = pltpu.roll(now, j, 0)
        for r in range(j):
            late = jnp.where(row == r, before[SHORT - 1 - j + r][None, :], late)
        total = total + taps_ref[i, SHORT - 1 - j : SHORT - j, :] * late
    return total


def grad_mm_kernel(at_ref, proj_ref, before_ref, taps_ref, cot0, cot1, cot2, cot3, *refs):
    *w_refs, out_ref, mixed_ref, sent_ref, cots_ref, buffer_ref, cot_sems, sems = refs
    copies = weight_copies(w_refs, buffer_ref, sems)
    arrivals = [
        piece_copy(ref, cots_ref.at[n], cot_sems, n) for n, ref in enumerate((cot0, cot1, cot2, cot3))
    ]
    for copy in arrivals + copies:
        copy.start()
    query = short_side(0, proj_ref, before_ref, taps_ref)
    for copy in arrivals:
        copy.wait()
    yl = at_ref[0]
    width = cot0.shape[2] // 2
    for place, (k, e) in enumerate(met_places(at_ref, -1)):
        if place % 2 == 0:
            for copy in copies[place * 2 : place * 2 + 4]:
                copy.wait()
        lhs = jnp.concatenate(
            [cots_ref[k, e, :, side_columns(at, width)] for at in (yl, 1 - yl)], axis=1
        )
        part = lax.dot_general(
            lhs,
            whole_columns(at_ref, place, buffer_ref),
            (((1,), (1,)), ((), ())),
            preferred_element_type=F32,
        )
        if place == 0:
            out_ref[...] = part
        else:
            out_ref[...] += part
    mixed = (out_ref[...] * query).astype(BF16)
    mixed_ref[...] = mixed
    sent_ref[...] = mixed.astype(F32).T.astype(BF16)


SCALARS = pl.BlockSpec(memory_space=pltpu.SMEM)
WHOLE = pl.BlockSpec(memory_space=pltpu.VMEM)
LEFT = pl.BlockSpec(memory_space=pl.ANY)


def grad_matmul(at, side_args, cots, ws):
    _, tok, rows = side_args[0].shape
    return pl.pallas_call(
        grad_mm_kernel,
        name="grad_matmul",
        out_shape=(
            OUTSIDE((tok, rows), F32),
            OUTSIDE((tok, rows), BF16),
            OUTSIDE((rows, tok), BF16),
        ),
        in_specs=[SCALARS] + [WHOLE] * len(side_args) + [LEFT] * (len(cots) + len(ws)),
        out_specs=(WHOLE,) * 3,
        scratch_shapes=[
            pltpu.VMEM((len(cots),) + cots[0].shape, BF16),
            pltpu.VMEM((len(ws),) + ws[0].shape, BF16),
            pltpu.SemaphoreType.DMA((len(cots),)),
            pltpu.SemaphoreType.DMA((len(ws),)),
        ],
        compiler_params=SCRATCH,
        cost_estimate=pl.CostEstimate(flops=4000000000, bytes_accessed=6500000, transcendentals=0),
    )(at, *side_args, *cots, *ws)


def mix_mm_kernel(at_ref, conv_ref, proj_ref, before_ref, taps_ref, skip_ref, grad_ref, *refs):
    *w_refs, out0, out1, out2, out3, query_grad_ref, parts_ref, buffer_ref, out_sems, sems = refs
    copies = weight_copies(w_refs, buffer_ref, sems)
    for copy in copies:
        copy.start()
    yl = at_ref[0]
    conv = conv_ref[...].astype(F32).T
    query, key, value = (short_side(i, proj_ref, before_ref, taps_ref) for i in range(3))
    mixed_in = conv + skip_ref[...] * (key * value).astype(BF16).astype(F32)
    query_grad_ref[...] = grad_ref[...] * mixed_in
    gated = (query * mixed_in).astype(BF16)
    width = parts_ref.shape[3] // 2
    for place, (k, e) in enumerate(met_places(at_ref, 1)):
        if place % 2 == 0:
            for copy in copies[place * 2 : place * 2 + 4]:
                copy.wait()
        part = jnp.dot(
            gated, whole_columns(at_ref, place, buffer_ref), preferred_element_type=F32
        ).astype(BF16)
        parts_ref[k, e, :, side_columns(yl, width)] = part[:, :width]
        parts_ref[k, e, :, side_columns(1 - yl, width)] = part[:, width:]
    leaving = [
        piece_copy(parts_ref.at[n], ref, out_sems, n) for n, ref in enumerate((out0, out1, out2, out3))
    ]
    for copy in leaving:
        copy.start()
    for copy in leaving:
        copy.wait()


def mix_matmul(at, conv, side_args, skip, grad, ws):
    tok, rows = grad.shape
    cols = 4 * ws[0].shape[-1]
    *parts, query_grad = pl.pallas_call(
        mix_mm_kernel,
        name="mix_matmul",
        out_shape=(OUTSIDE((2, tok, cols), BF16),) * 4 + (OUTSIDE((tok, rows), F32),),
        in_specs=[SCALARS] + [WHOLE] * (3 + len(side_args)) + [LEFT] * len(ws),
        out_specs=(LEFT,) * 4 + (WHOLE,),
        scratch_shapes=[
            pltpu.VMEM((4, 2, tok, cols), BF16),
            pltpu.VMEM((len(ws),) + ws[0].shape, BF16),
            pltpu.SemaphoreType.DMA((4,)),
            pltpu.SemaphoreType.DMA((len(ws),)),
        ],
        compiler_params=SCRATCH,
        cost_estimate=pl.CostEstimate(flops=4000000000, bytes_accessed=6500000, transcendentals=0),
    )(at, conv, *side_args, outside(skip), outside(grad), *ws)
    return parts, query_grad


def shift_z(shard, by):
    count = lax.axis_size("z")
    return lax.ppermute(shard, "z", [(i, (i + by) % count) for i in range(count)])


def cross_z(shard, by):
    return lax.ppermute(shard, "z", [(i, i ^ by) for i in range(lax.axis_size("z"))])


def shift_x(shard, by):
    count = lax.axis_size("x")
    return lax.ppermute(shard, "x", [(i, (i + by) % count) for i in range(count)])


def pre_kernel(proj_ref, before_ref, taps_ref, sent_ref):
    key, value = (short_side(i, proj_ref, before_ref, taps_ref) for i in (1, 2))
    sent_ref[...] = (key * value).T.astype(BF16)


def carried_columns(side_args):
    _, tok, cols = side_args[0].shape
    return pl.pallas_call(
        pre_kernel,
        name="carried_columns",
        out_shape=OUTSIDE((cols, tok), BF16),
        compiler_params=SCRATCH,
        cost_estimate=pl.CostEstimate(flops=5000000, bytes_accessed=1500000, transcendentals=0),
    )(*side_args)


def final_kernel(
    back_ref, mixed_ref, query_grad_ref, proj_ref, before_ref, taps_ref, skip_ref, out_ref, head_ref, tail_ref
):
    tok = mixed_ref.shape[0]
    row = lax.broadcasted_iota(jnp.int32, mixed_ref.shape, 0)
    carried_grad = back_ref[...].astype(F32).T + skip_ref[...] * mixed_ref[...].astype(F32)
    key, value = (short_side(i, proj_ref, before_ref, taps_ref) for i in (1, 2))
    grads = (query_grad_ref[...], carried_grad * value, carried_grad * key)
    for i, grad in enumerate(grads):
        head_ref[i] = grad[: head_ref.shape[1]]
        total = taps_ref[i, SHORT - 1 : SHORT, :] * grad
        for j in range(1, SHORT):
            early = jnp.where(row < tok - j, pltpu.roll(grad, tok - j, 0), 0.0)
            total = total + taps_ref[i, SHORT - 1 - j : SHORT - j, :] * early
        out_ref[i] = total.astype(BF16)
        tail_ref[i] = total[tok - EDGE :]


def final_short(back, mixed_grad, query_grad, side_args, skip):
    tok, cols = mixed_grad.shape
    return pl.pallas_call(
        final_kernel,
        name="final_short",
        out_shape=(
            jax.ShapeDtypeStruct((3, tok, cols), BF16),
            OUTSIDE((3, 8, cols), F32),
            jax.ShapeDtypeStruct((3, EDGE, cols), F32),
        ),
        compiler_params=SCRATCH,
        cost_estimate=pl.CostEstimate(flops=5000000, bytes_accessed=3500000, transcendentals=0),
    )(back, outside(mixed_grad), outside(query_grad), *side_args, skip)


def edge_kernel(tail_ref, after_ref, taps_ref, whole_ref, out_ref):
    row = lax.broadcasted_iota(jnp.int32, tail_ref.shape[1:], 0)
    for i in range(3):
        after = after_ref[i]
        total = tail_ref[i]
        for s in range(SHORT - 1):
            missing = sum(
                taps_ref[i, SHORT - 2 - s - r : SHORT - 1 - s - r, :] * after[r : r + 1]
                for r in range(SHORT - 1 - s)
            )
            total = total + jnp.where(row == EDGE - 1 - s, 1.0, 0.0) * missing
        out_ref[i] = total.astype(BF16)


def edge_rows(tail, after, taps, whole):
    _, tok, cols = whole.shape
    return pl.pallas_call(
        edge_kernel,
        name="edge_rows",
        out_shape=jax.ShapeDtypeStruct(whole.shape, BF16),
        grid=(1,),
        in_specs=[
            pl.BlockSpec(tail.shape, lambda i: (0, 0, 0)),
            pl.BlockSpec(after.shape, lambda i: (0, 0, 0)),
            pl.BlockSpec(taps.shape, lambda i: (0, 0, 0)),
            pl.BlockSpec(memory_space=pl.ANY),
        ],
        out_specs=pl.BlockSpec((3, EDGE, cols), lambda i: (0, tok // EDGE - 1, 0)),
        input_output_aliases={3: 0},
        compiler_params=SCRATCH,
        cost_estimate=pl.CostEstimate(flops=500000, bytes_accessed=200000, transcendentals=0),
    )(tail, after, taps, whole)


def channel_major(sent):
    count = lax.axis_size(SEQ)
    sent = sent.reshape(count, sent.shape[0] // count, sent.shape[1])
    return lax.all_to_all(sent, SEQ, split_axis=0, concat_axis=0, tiled=True)


def token_major(block):
    got = lax.all_to_all(block, SEQ, split_axis=0, concat_axis=0, tiled=True)
    return got.reshape(got.shape[0] * got.shape[1], got.shape[2])


def on_device(projected, short_weight, filters, skip, out_weight, cotangent):
    tok_rows, _ = cotangent.shape
    groups_dev, seq_length = filters.shape
    rim = SHORT - 1
    wide, deep = lax.axis_size("x"), lax.axis_size("z")
    yl, core = lax.axis_index("yl"), lax.axis_index("core")
    yh, x, z = lax.axis_index("yh"), lax.axis_index("x"), lax.axis_index("z")

    at = jnp.stack([yl, core, yh, x, z]).astype(jnp.int32)
    before = from_behind(projected[tok_rows - rim :], 1)
    cot_pair = jnp.stack([cotangent, swap(cotangent, "yh")])
    cots = [cot_pair] + [shift_x(cot_pair, k) for k in range(1, wide)]
    w_pair = jnp.stack([out_weight, cross_z(out_weight, 4)])
    pairs = [shift_z(w_pair, deep - 1), shift_z(w_pair, 1), cross_z(w_pair, 2)]
    sides = [swap(w_pair, "yl")]
    sides += [swap(p, "yl") for p in pairs]
    pairs = [w_pair] + pairs
    pairs_c = [swap(p, "core") for p in pairs]
    sides_c = [swap(p, "core") for p in sides]
    ws = tuple(w for group in zip(pairs, pairs_c, sides, sides_c) for w in group)

    side_args = (projected.transpose(1, 0, 2), before.transpose(1, 0, 2), short_weight)
    carried_sent = carried_columns((outside(side_args[0]), side_args[1], outside(side_args[2])))
    carried_seq = channel_major(carried_sent)
    conv_seq = conv_forward(carried_seq, filters)
    conv = token_major(conv_seq)

    gated_grad, mixed_grad, grad_sent = grad_matmul(at, side_args, cots, ws)
    grad_seq = channel_major(grad_sent)

    parts, query_grad = mix_matmul(at, conv, side_args, skip[None, :], gated_grad, ws)
    shares = [parts[0]] + [shift_x(parts[k], k) for k in range(1, wide)]
    theirs = sum(p[1].astype(F32) for p in shares).astype(BF16)
    mine = sum(p[0].astype(F32) for p in shares)
    theirs, mine = lax.optimization_barrier((theirs, mine))
    got = swap(theirs, "yh")
    mixed = (mine + got.astype(F32)).astype(BF16)

    back_seq, filter_grad = conv_backward(grad_seq, carried_seq, filters)
    back = token_major(back_seq)
    whole, head, tail = final_short(back, mixed_grad, query_grad, side_args, skip[None, :])
    after = from_behind(head, -1)
    projected_grad = edge_rows(tail, after, short_weight, whole)
    return (
        mixed,
        projected_grad.transpose(1, 0, 2),
        filter_grad.reshape(groups_dev, seq_length),
    )


def solution(mesh):
    fine = Mesh(mesh.devices.reshape(8, 2, 2, 2, 4), ("z", "yl", "core", "yh", "x"))
    placed = (
        P(SEQ, None, CHAN),
        P(None, None, CHAN),
        P(CHAN + SEQ, None),
        P(CHAN),
        P(CHAN, SEQ),
        P(SEQ, CHAN),
    )
    return jax.shard_map(
        on_device,
        mesh=fine,
        in_specs=placed,
        out_specs=(P(SEQ, CHAN), P(SEQ, None, CHAN), P(CHAN + SEQ, None)),
        check_vma=False,
    )
```

```python
import functools
import math

import jax
import jax.numpy as jnp
from jax import lax
from jax.experimental import pallas as pl
from jax.experimental.pallas import tpu as pltpu
from jax.sharding import Mesh, PartitionSpec as P


GROUP = 8
SHORT = 3
BLOCK = 256
HALF = 128
LAGS = 4
SCRATCH = pltpu.CompilerParams(vmem_limit_bytes=24 << 20)
BUILD_UNROLL = 16
EDGE = 16
OUTSIDE = pltpu.HBM

SEQ = ("z", "yl", "core")
CHAN = ("yh", "x")
F32 = jnp.float32
BF16 = jnp.bfloat16


def from_behind(shard, by):
    count = lax.axis_size(SEQ)
    pairs = [(i, i + by) for i in range(count) if 0 <= i + by < count]
    return lax.ppermute(shard, SEQ, pairs)


def swap(shard, axis):
    return lax.ppermute(shard, axis, [(0, 1), (1, 0)])


def skew_masks():
    rows = lax.broadcasted_iota(jnp.int32, (HALF, HALF), 0)
    lanes = lax.broadcasted_iota(jnp.int32, (HALF, HALF), 1)
    return rows, lanes


def build_tiles(h_ref, tile_ref):
    groups, count = tile_ref.shape[0], tile_ref.shape[1] - 1
    rows, lanes = skew_masks()
    inside = lanes >= rows
    zero = jnp.zeros((HALF, HALF), F32)
    for g in range(groups):
        tile_ref[g, 0] = zero.astype(BF16)

    def step(j, before):
        turns = []
        for g in range(groups):
            row = h_ref[g : g + 1, pl.ds(pl.multiple_of(j * HALF, HALF), HALF)]
            turned = pltpu.roll(jnp.broadcast_to(row, (HALF, HALF)), 0, 1, stride=1, stride_axis=0)
            tile_ref[g, j + 1] = jnp.where(inside, turned, before[g]).astype(BF16)
            turns.append(turned)
        return tuple(turns)

    lax.fori_loop(0, count, step, (zero,) * groups, unroll=BUILD_UNROLL)


def toeplitz_block(tile_ref, g, d):
    same = tile_ref[g, 2 * d + 1]
    upper = jnp.concatenate([same, tile_ref[g, 2 * d + 2]], axis=1)
    lower = jnp.concatenate([tile_ref[g, 2 * d], same], axis=1)
    return jnp.concatenate([upper, lower], axis=0)


def group_rows(ref, g):
    part = ref[...].astype(F32)[:, g * GROUP : (g + 1) * GROUP, :]
    return part.reshape(part.shape[0] * GROUP, BLOCK)


def conv_kernel(x_ref, h_ref, y_ref, tile_ref, wide_ref, acc_ref):
    blocks, chans, _ = x_ref.shape
    total = blocks * GROUP
    parts = []
    build_tiles(h_ref, tile_ref)
    for g in range(chans // GROUP):
        signal = group_rows(x_ref, g)
        for k in range(LAGS):
            late = signal
            if k > 0:
                late = jnp.concatenate(
                    [jnp.zeros((k * GROUP, BLOCK), F32), signal[: total - k * GROUP]], axis=0
                )
            wide_ref[:, k * BLOCK : (k + 1) * BLOCK] = late.astype(BF16)
        for d in range(0, blocks, LAGS):
            rows = total - d * GROUP
            weights = jnp.concatenate(
                [toeplitz_block(tile_ref, g, d + k) for k in range(LAGS)], axis=0
            )
            part = jnp.dot(wide_ref[:rows, :], weights, preferred_element_type=F32)
            if d == 0:
                acc_ref[...] = part
            else:
                acc_ref[d * GROUP :, :] += part
        parts.append(acc_ref[...].reshape(blocks, GROUP, BLOCK))
    y_ref[...] = jnp.concatenate(parts, axis=1).astype(BF16)


def back_kernel(m_ref, x_ref, h_ref, y_ref, f_ref, tile_ref, wide_ref, acc_ref, low_ref, high_ref, *, scale):
    blocks, chans, _ = x_ref.shape
    total = blocks * GROUP
    rows_i, lanes_i = skew_masks()
    wrapped = lanes_i <= rows_i
    flip = (
        lax.broadcasted_iota(jnp.int32, (BLOCK, BLOCK), 0)
        + lax.broadcasted_iota(jnp.int32, (BLOCK, BLOCK), 1)
        == BLOCK - 1
    )
    flip = jnp.where(flip, 1.0, 0.0).astype(BF16)
    zero = jnp.zeros((HALF, HALF), F32)
    build_tiles(h_ref, tile_ref)
    parts = []

    def fold(v):
        return v.reshape(HALF // 8, 8, HALF).sum(axis=0)

    def turned(cross, r, l):
        return pltpu.roll(
            cross[r * HALF : (r + 1) * HALF, l * HALF : (l + 1) * HALF], 1, 1, stride=1, stride_axis=0
        )

    for g in range(chans // GROUP):
        grad = group_rows(m_ref, g)
        wide_ref[total:, :] = jnp.zeros((wide_ref.shape[0] - total, LAGS * BLOCK), BF16)
        for k in range(LAGS):
            early = grad
            if k > 0:
                early = jnp.concatenate(
                    [grad[k * GROUP :], jnp.zeros((k * GROUP, BLOCK), F32)], axis=0
                )
            wide_ref[:total, k * BLOCK : (k + 1) * BLOCK] = early.astype(BF16)
        signal = group_rows(x_ref, g).astype(BF16)
        flipped = lax.dot_general(
            flip, signal, (((1,), (1,)), ((), ())), preferred_element_type=F32
        ).astype(BF16)
        high_ref[blocks] = jnp.zeros((8, BLOCK), F32)
        for d in range(0, blocks, LAGS):
            rows = total - d * GROUP
            weights = jnp.concatenate(
                [toeplitz_block(tile_ref, g, d + k) for k in range(LAGS)], axis=1
            )
            part = lax.dot_general(
                wide_ref[d * GROUP : total, :],
                weights,
                (((1,), (1,)), ((), ())),
                preferred_element_type=F32,
            )
            if d == 0:
                acc_ref[...] = part
            else:
                acc_ref[:rows, :] += part
            depth = total if 2 * d < blocks else total // 2
            cross_all = jnp.dot(
                flipped[:, :depth],
                wide_ref[d * GROUP : d * GROUP + depth, :],
                preferred_element_type=F32,
            )
            for k in range(LAGS):
                cross = cross_all[:, k * BLOCK : (k + 1) * BLOCK]
                s00, s01, s10, s11 = (turned(cross, r, l) for r in range(2) for l in range(2))
                low0 = jnp.where(wrapped, s01 + s10, s11)
                high0 = jnp.where(wrapped, zero, s00)
                low1 = jnp.where(wrapped, s11, zero)
                high1 = jnp.where(wrapped, s00, s01 + s10)
                low_ref[d + k] = jnp.concatenate([fold(low0), fold(low1)], axis=1)
                high_ref[d + k] = jnp.concatenate([fold(high0), fold(high1)], axis=1)
        parts.append(acc_ref[...].reshape(blocks, GROUP, BLOCK))
        rows = (low_ref[...] + high_ref[pl.ds(1, blocks)]).sum(axis=1) * scale
        for d in range(blocks):
            f_ref[g : g + 1, d * BLOCK : (d + 1) * BLOCK] = rows[d : d + 1]
    y_ref[...] = jnp.concatenate(parts, axis=1).astype(BF16)


def conv_forward(x, h):
    blocks = x.shape[0]
    total = blocks * GROUP
    return pl.pallas_call(
        conv_kernel,
        name="conv_forward",
        out_shape=jax.ShapeDtypeStruct(x.shape, BF16),
        scratch_shapes=[
            pltpu.VMEM((h.shape[0], h.shape[1] // HALF + 1, HALF, HALF), BF16),
            pltpu.VMEM((total, LAGS * BLOCK), BF16),
            pltpu.VMEM((total, BLOCK), F32),
        ],
        compiler_params=SCRATCH,
        cost_estimate=pl.CostEstimate(flops=6000000000, bytes_accessed=600000, transcendentals=0),
    )(x, h)


def conv_backward(m, x, h):
    blocks, chans, _ = x.shape
    total = blocks * GROUP
    scale = 1.0 / math.sqrt(GROUP * blocks * BLOCK)
    return pl.pallas_call(
        functools.partial(back_kernel, scale=scale),
        name="conv_backward",
        out_shape=(
            jax.ShapeDtypeStruct(x.shape, BF16),
            jax.ShapeDtypeStruct((chans // GROUP, blocks * BLOCK), F32),
        ),
        scratch_shapes=[
            pltpu.VMEM((h.shape[0], h.shape[1] // HALF + 1, HALF, HALF), BF16),
            pltpu.VMEM((total + total // 2, LAGS * BLOCK), BF16),
            pltpu.VMEM((total, BLOCK), F32),
            pltpu.VMEM((blocks, 8, BLOCK), F32),
            pltpu.VMEM((blocks + 1, 8, BLOCK), F32),
        ],
        compiler_params=SCRATCH,
        cost_estimate=pl.CostEstimate(flops=10000000000, bytes_accessed=1000000, transcendentals=0),
    )(m, x, h)


def met_places(at_ref, sign):
    z = at_ref[4]
    for first in (z, (z + 1) & 7, (z + 7) & 7, z ^ 2):
        for chan in (first, first ^ 4):
            yield (sign * ((chan & 3) - at_ref[3])) & 3, (chan >> 2) ^ at_ref[2]


def outside(array):
    return pltpu.with_memory_space_constraint(array, pltpu.HBM)


def piece_copy(source, target, sems, n):
    return pltpu.make_async_copy(source, target, sems.at[n])


def weight_copies(refs, buffer_ref, sems):
    return [piece_copy(ref, buffer_ref.at[n], sems, n) for n, ref in enumerate(refs)]


def all_columns(at_ref, pair, half, buffer_ref):
    first = at_ref[1] == 0
    own, own_c, side, side_c = (buffer_ref[pair * 4 + n, half] for n in range(4))
    parts = []
    for mine, other in ((own, own_c), (side, side_c)):
        parts += [jnp.where(first, mine, other), jnp.where(first, other, mine)]
    return jnp.concatenate(parts, axis=1)


def met_columns(at_ref, k, e, buffer_ref):
    z = at_ref[4]
    chan = ((at_ref[2] + e) & 1) * 4 + ((at_ref[3] + k) & 3)
    apart = (chan - z) & 3
    pair = jnp.where(apart == 0, 0, jnp.where(apart == 1, 1, jnp.where(apart == 3, 2, 3)))
    start = jnp.where(pair == 3, z ^ 2, (z + jnp.where(pair == 2, 7, pair)) & 7)
    return all_columns(at_ref, pair, jnp.where(chan == start, 0, 1), buffer_ref)


def side_columns(side, width):
    return pl.ds(pl.multiple_of(side * width, width), width)


def short_side(i, proj_ref, before_ref, taps_ref):
    now = proj_ref[i].astype(F32)
    before = before_ref[i].astype(F32)
    row = lax.broadcasted_iota(jnp.int32, now.shape, 0)
    total = taps_ref[i, SHORT - 1 : SHORT, :] * now
    for j in range(1, SHORT):
        late = pltpu.roll(now, j, 0)
        for r in range(j):
            late = jnp.where(row == r, before[SHORT - 1 - j + r][None, :], late)
        total = total + taps_ref[i, SHORT - 1 - j : SHORT - j, :] * late
    return total


def grad_mm_kernel(at_ref, proj_ref, before_ref, taps_ref, cot0, cot1, cot2, cot3, *refs):
    *w_refs, out_ref, mixed_ref, sent_ref, cots_ref, buffer_ref, cot_sems, sems = refs
    copies = weight_copies(w_refs, buffer_ref, sems)
    arrivals = [
        piece_copy(ref, cots_ref.at[n], cot_sems, n) for n, ref in enumerate((cot0, cot1, cot2, cot3))
    ]
    for copy in arrivals + copies:
        copy.start()
    query = short_side(0, proj_ref, before_ref, taps_ref)
    for copy in arrivals:
        copy.wait()
    yl = at_ref[0]
    width = cot0.shape[2] // 2
    for place, (k, e) in enumerate(met_places(at_ref, -1)):
        if place % 2 == 0:
            for copy in copies[place * 2 : place * 2 + 4]:
                copy.wait()
        lhs = jnp.concatenate(
            [cots_ref[k, e, :, side_columns(at, width)] for at in (yl, 1 - yl)], axis=1
        )
        part = lax.dot_general(
            lhs,
            all_columns(at_ref, place // 2, place % 2, buffer_ref),
            (((1,), (1,)), ((), ())),
            preferred_element_type=F32,
        )
        if place == 0:
            out_ref[...] = part
        else:
            out_ref[...] += part
    mixed = (out_ref[...] * query).astype(BF16)
    mixed_ref[...] = mixed
    sent_ref[...] = mixed.astype(F32).T.astype(BF16)


SCALARS = pl.BlockSpec(memory_space=pltpu.SMEM)
WHOLE = pl.BlockSpec(memory_space=pltpu.VMEM)
LEFT = pl.BlockSpec(memory_space=pl.ANY)


def grad_matmul(at, side_args, cots, ws):
    _, tok, rows = side_args[0].shape
    return pl.pallas_call(
        grad_mm_kernel,
        name="grad_matmul",
        out_shape=(
            OUTSIDE((tok, rows), F32),
            OUTSIDE((tok, rows), BF16),
            OUTSIDE((rows, tok), BF16),
        ),
        in_specs=[SCALARS] + [WHOLE] * len(side_args) + [LEFT] * (len(cots) + len(ws)),
        out_specs=(WHOLE,) * 3,
        scratch_shapes=[
            pltpu.VMEM((len(cots),) + cots[0].shape, BF16),
            pltpu.VMEM((len(ws),) + ws[0].shape, BF16),
            pltpu.SemaphoreType.DMA((len(cots),)),
            pltpu.SemaphoreType.DMA((len(ws),)),
        ],
        compiler_params=SCRATCH,
        cost_estimate=pl.CostEstimate(flops=4000000000, bytes_accessed=6500000, transcendentals=0),
    )(at, *side_args, *cots, *ws)


def mix_mm_kernel(at_ref, conv_ref, proj_ref, before_ref, taps_ref, skip_ref, grad_ref, *refs):
    *w_refs, out0, out1, out2, out3, query_grad_ref, parts_ref, buffer_ref, out_sems, sems = refs
    copies = weight_copies(w_refs, buffer_ref, sems)
    for copy in copies:
        copy.start()
    yl = at_ref[0]
    conv = conv_ref[...].astype(F32).T
    query, key, value = (short_side(i, proj_ref, before_ref, taps_ref) for i in range(3))
    mixed_in = conv + skip_ref[...] * (key * value).astype(BF16).astype(F32)
    query_grad_ref[...] = grad_ref[...] * mixed_in
    gated = (query * mixed_in).astype(BF16)
    width = parts_ref.shape[3] // 2
    for copy in copies:
        copy.wait()
    leaving = []
    for k, ref in enumerate((out0, out1, out2, out3)):
        for e in range(2):
            part = jnp.dot(
                gated, met_columns(at_ref, k, e, buffer_ref), preferred_element_type=F32
            ).astype(BF16)
            parts_ref[k, e, :, side_columns(yl, width)] = part[:, :width]
            parts_ref[k, e, :, side_columns(1 - yl, width)] = part[:, width:]
        leaving.append(piece_copy(parts_ref.at[k], ref, out_sems, k))
        leaving[-1].start()
    for copy in leaving:
        copy.wait()


def mix_matmul(at, conv, side_args, skip, grad, ws):
    tok, rows = grad.shape
    cols = 4 * ws[0].shape[-1]
    *parts, query_grad = pl.pallas_call(
        mix_mm_kernel,
        name="mix_matmul",
        out_shape=(OUTSIDE((2, tok, cols), BF16),) * 4 + (OUTSIDE((tok, rows), F32),),
        in_specs=[SCALARS] + [WHOLE] * (3 + len(side_args)) + [LEFT] * len(ws),
        out_specs=(LEFT,) * 4 + (WHOLE,),
        scratch_shapes=[
            pltpu.VMEM((4, 2, tok, cols), BF16),
            pltpu.VMEM((len(ws),) + ws[0].shape, BF16),
            pltpu.SemaphoreType.DMA((4,)),
            pltpu.SemaphoreType.DMA((len(ws),)),
        ],
        compiler_params=SCRATCH,
        cost_estimate=pl.CostEstimate(flops=4000000000, bytes_accessed=6500000, transcendentals=0),
    )(at, conv, *side_args, outside(skip), outside(grad), *ws)
    return parts, query_grad


def shift_z(shard, by):
    count = lax.axis_size("z")
    return lax.ppermute(shard, "z", [(i, (i + by) % count) for i in range(count)])


def cross_z(shard, by):
    return lax.ppermute(shard, "z", [(i, i ^ by) for i in range(lax.axis_size("z"))])


def shift_x(shard, by):
    count = lax.axis_size("x")
    return lax.ppermute(shard, "x", [(i, (i + by) % count) for i in range(count)])


def pre_kernel(proj_ref, before_ref, taps_ref, sent_ref):
    key, value = (short_side(i, proj_ref, before_ref, taps_ref) for i in (1, 2))
    sent_ref[...] = (key * value).T.astype(BF16)


def carried_columns(side_args):
    _, tok, cols = side_args[0].shape
    return pl.pallas_call(
        pre_kernel,
        name="carried_columns",
        out_shape=OUTSIDE((cols, tok), BF16),
        compiler_params=SCRATCH,
        cost_estimate=pl.CostEstimate(flops=5000000, bytes_accessed=1500000, transcendentals=0),
    )(*side_args)


def final_kernel(
    back_ref, mixed_ref, query_grad_ref, proj_ref, before_ref, taps_ref, skip_ref, out_ref, head_ref, tail_ref
):
    tok = mixed_ref.shape[0]
    row = lax.broadcasted_iota(jnp.int32, mixed_ref.shape, 0)
    carried_grad = back_ref[...].astype(F32).T + skip_ref[...] * mixed_ref[...].astype(F32)
    key, value = (short_side(i, proj_ref, before_ref, taps_ref) for i in (1, 2))
    grads = (query_grad_ref[...], carried_grad * value, carried_grad * key)
    for i, grad in enumerate(grads):
        head_ref[i] = grad[: head_ref.shape[1]]
        total = taps_ref[i, SHORT - 1 : SHORT, :] * grad
        for j in range(1, SHORT):
            early = jnp.where(row < tok - j, pltpu.roll(grad, tok - j, 0), 0.0)
            total = total + taps_ref[i, SHORT - 1 - j : SHORT - j, :] * early
        out_ref[i] = total.astype(BF16)
        tail_ref[i] = total[tok - EDGE :]


def final_short(back, mixed_grad, query_grad, side_args, skip):
    tok, cols = mixed_grad.shape
    return pl.pallas_call(
        final_kernel,
        name="final_short",
        out_shape=(
            jax.ShapeDtypeStruct((3, tok, cols), BF16),
            OUTSIDE((3, 8, cols), F32),
            jax.ShapeDtypeStruct((3, EDGE, cols), F32),
        ),
        compiler_params=SCRATCH,
        cost_estimate=pl.CostEstimate(flops=5000000, bytes_accessed=3500000, transcendentals=0),
    )(back, mixed_grad, query_grad, *side_args, outside(skip))


def edge_kernel(tail_ref, after_ref, taps_ref, whole_ref, out_ref):
    row = lax.broadcasted_iota(jnp.int32, tail_ref.shape[1:], 0)
    for i in range(3):
        after = after_ref[i]
        total = tail_ref[i]
        for s in range(SHORT - 1):
            missing = sum(
                taps_ref[i, SHORT - 2 - s - r : SHORT - 1 - s - r, :] * after[r : r + 1]
                for r in range(SHORT - 1 - s)
            )
            total = total + jnp.where(row == EDGE - 1 - s, 1.0, 0.0) * missing
        out_ref[i] = total.astype(BF16)


def edge_rows(tail, after, taps, whole):
    _, tok, cols = whole.shape
    return pl.pallas_call(
        edge_kernel,
        name="edge_rows",
        out_shape=jax.ShapeDtypeStruct(whole.shape, BF16),
        grid=(1,),
        in_specs=[
            pl.BlockSpec(tail.shape, lambda i: (0, 0, 0)),
            pl.BlockSpec(after.shape, lambda i: (0, 0, 0)),
            pl.BlockSpec(taps.shape, lambda i: (0, 0, 0)),
            pl.BlockSpec(memory_space=pl.ANY),
        ],
        out_specs=pl.BlockSpec((3, EDGE, cols), lambda i: (0, tok // EDGE - 1, 0)),
        input_output_aliases={3: 0},
        compiler_params=SCRATCH,
        cost_estimate=pl.CostEstimate(flops=500000, bytes_accessed=200000, transcendentals=0),
    )(tail, after, taps, whole)


def channel_major(sent):
    count = lax.axis_size(SEQ)
    sent = sent.reshape(count, sent.shape[0] // count, sent.shape[1])
    return lax.all_to_all(sent, SEQ, split_axis=0, concat_axis=0, tiled=True)


def token_major(block):
    got = lax.all_to_all(block, SEQ, split_axis=0, concat_axis=0, tiled=True)
    return got.reshape(got.shape[0] * got.shape[1], got.shape[2])


def on_device(projected, short_weight, filters, skip, out_weight, cotangent):
    tok_rows, _ = cotangent.shape
    rim = SHORT - 1
    wide, deep = lax.axis_size("x"), lax.axis_size("z")
    yl, core = lax.axis_index("yl"), lax.axis_index("core")
    yh, x, z = lax.axis_index("yh"), lax.axis_index("x"), lax.axis_index("z")

    at = jnp.stack([yl, core, yh, x, z]).astype(jnp.int32)
    before = from_behind(projected[tok_rows - rim :], 1)
    cot_pair = jnp.stack([cotangent, swap(cotangent, "yh")])
    cots = [cot_pair] + [shift_x(cot_pair, k) for k in range(1, wide)]
    w_pair = jnp.stack([out_weight, cross_z(out_weight, 4)])
    pairs = [shift_z(w_pair, deep - 1), shift_z(w_pair, 1), cross_z(w_pair, 2)]
    sides = [swap(w_pair, "yl")]
    sides += [swap(p, "yl") for p in pairs]
    pairs = [w_pair] + pairs
    pairs_c = [swap(p, "core") for p in pairs]
    sides_c = [swap(p, "core") for p in sides]
    ws = tuple(w for group in zip(pairs, pairs_c, sides, sides_c) for w in group)

    side_args = (projected.transpose(1, 0, 2), before.transpose(1, 0, 2), short_weight)
    carried_sent = carried_columns((outside(side_args[0]), side_args[1], outside(side_args[2])))
    carried_seq = channel_major(carried_sent)
    conv_seq = conv_forward(carried_seq, filters)
    conv = token_major(conv_seq)

    gated_grad, mixed_grad, grad_sent = grad_matmul(at, side_args, cots, ws)
    grad_seq = channel_major(grad_sent)

    parts, query_grad = mix_matmul(at, conv, side_args, skip[None, :], gated_grad, ws)
    shares = [parts[0]] + [shift_x(parts[k], k) for k in range(1, wide)]
    theirs = sum(p[1].astype(F32) for p in shares).astype(BF16)
    mine = sum(p[0].astype(F32) for p in shares)
    theirs, mine = lax.optimization_barrier((theirs, mine))
    got = swap(theirs, "yh")
    mixed = (mine + got.astype(F32)).astype(BF16)

    back_seq, filter_grad = conv_backward(grad_seq, carried_seq, filters)
    back = token_major(back_seq)
    whole, head, tail = final_short(back, mixed_grad, query_grad, side_args, skip[None, :])
    after = from_behind(head, -1)
    projected_grad = edge_rows(tail, after, short_weight, whole)
    return (
        mixed,
        projected_grad.transpose(1, 0, 2),
        filter_grad,
    )


def solution(mesh):
    fine = Mesh(mesh.devices.reshape(8, 2, 2, 2, 4), ("z", "yl", "core", "yh", "x"))
    placed = (
        P(SEQ, None, CHAN),
        P(None, None, CHAN),
        P(CHAN + SEQ, None),
        P(CHAN),
        P(CHAN, SEQ),
        P(SEQ, CHAN),
    )
    return jax.shard_map(
        on_device,
        mesh=fine,
        in_specs=placed,
        out_specs=(P(SEQ, CHAN), P(SEQ, None, CHAN), P(CHAN + SEQ, None)),
        check_vma=False,
    )
```

```python
import functools
import math

import jax
import jax.numpy as jnp
from jax import lax
from jax.experimental import pallas as pl
from jax.experimental.pallas import tpu as pltpu
from jax.sharding import Mesh, PartitionSpec as P


GROUP = 8
SHORT = 3
BLOCK = 256
HALF = 128
LAGS = 4
SCRATCH = pltpu.CompilerParams(vmem_limit_bytes=24 << 20)
BUILD_UNROLL = 16
EDGE = 16
OUTSIDE = pltpu.HBM

SEQ = ("z", "yl", "core")
CHAN = ("yh", "x")
F32 = jnp.float32
BF16 = jnp.bfloat16


def from_behind(shard, by):
    count = lax.axis_size(SEQ)
    pairs = [(i, i + by) for i in range(count) if 0 <= i + by < count]
    return lax.ppermute(shard, SEQ, pairs)


def swap(shard, axis):
    return lax.ppermute(shard, axis, [(0, 1), (1, 0)])


def skew_masks():
    rows = lax.broadcasted_iota(jnp.int32, (HALF, HALF), 0)
    lanes = lax.broadcasted_iota(jnp.int32, (HALF, HALF), 1)
    return rows, lanes


def build_tiles(h_ref, tile_ref):
    groups, count = tile_ref.shape[0], tile_ref.shape[1] - 1
    rows, lanes = skew_masks()
    inside = lanes >= rows
    zero = jnp.zeros((HALF, HALF), F32)
    for g in range(groups):
        tile_ref[g, 0] = zero.astype(BF16)

    def step(j, before):
        turns = []
        for g in range(groups):
            row = h_ref[g : g + 1, pl.ds(pl.multiple_of(j * HALF, HALF), HALF)]
            turned = pltpu.roll(jnp.broadcast_to(row, (HALF, HALF)), 0, 1, stride=1, stride_axis=0)
            tile_ref[g, j + 1] = jnp.where(inside, turned, before[g]).astype(BF16)
            turns.append(turned)
        return tuple(turns)

    lax.fori_loop(0, count, step, (zero,) * groups, unroll=BUILD_UNROLL)


def toeplitz_block(tile_ref, g, d):
    same = tile_ref[g, 2 * d + 1]
    upper = jnp.concatenate([same, tile_ref[g, 2 * d + 2]], axis=1)
    lower = jnp.concatenate([tile_ref[g, 2 * d], same], axis=1)
    return jnp.concatenate([upper, lower], axis=0)


def group_rows(ref, g):
    part = ref[...].astype(F32)[:, g * GROUP : (g + 1) * GROUP, :]
    return part.reshape(part.shape[0] * GROUP, BLOCK)


def conv_kernel(x_ref, h_ref, y_ref, tile_ref, wide_ref, acc_ref):
    blocks, chans, _ = x_ref.shape
    total = blocks * GROUP
    parts = []
    build_tiles(h_ref, tile_ref)
    for g in range(chans // GROUP):
        signal = group_rows(x_ref, g)
        for k in range(LAGS):
            late = signal
            if k > 0:
                late = jnp.concatenate(
                    [jnp.zeros((k * GROUP, BLOCK), F32), signal[: total - k * GROUP]], axis=0
                )
            wide_ref[:, k * BLOCK : (k + 1) * BLOCK] = late.astype(BF16)
        for d in range(0, blocks, LAGS):
            rows = total - d * GROUP
            weights = jnp.concatenate(
                [toeplitz_block(tile_ref, g, d + k) for k in range(LAGS)], axis=0
            )
            part = jnp.dot(wide_ref[:rows, :], weights, preferred_element_type=F32)
            if d == 0:
                acc_ref[...] = part
            else:
                acc_ref[d * GROUP :, :] += part
        parts.append(acc_ref[...].reshape(blocks, GROUP, BLOCK))
    y_ref[...] = jnp.concatenate(parts, axis=1).astype(BF16)


def back_kernel(m_ref, x_ref, h_ref, y_ref, f_ref, tile_ref, wide_ref, acc_ref, low_ref, high_ref, *, scale):
    blocks, chans, _ = x_ref.shape
    total = blocks * GROUP
    rows_i, lanes_i = skew_masks()
    wrapped = lanes_i <= rows_i
    flip = (
        lax.broadcasted_iota(jnp.int32, (BLOCK, BLOCK), 0)
        + lax.broadcasted_iota(jnp.int32, (BLOCK, BLOCK), 1)
        == BLOCK - 1
    )
    flip = jnp.where(flip, 1.0, 0.0).astype(BF16)
    zero = jnp.zeros((HALF, HALF), F32)
    build_tiles(h_ref, tile_ref)
    parts = []

    def fold(v):
        return v.reshape(HALF // 8, 8, HALF).sum(axis=0)

    def turned(cross, r, l):
        return pltpu.roll(
            cross[r * HALF : (r + 1) * HALF, l * HALF : (l + 1) * HALF], 1, 1, stride=1, stride_axis=0
        )

    for g in range(chans // GROUP):
        grad = group_rows(m_ref, g)
        wide_ref[total:, :] = jnp.zeros((wide_ref.shape[0] - total, LAGS * BLOCK), BF16)
        for k in range(LAGS):
            early = grad
            if k > 0:
                early = jnp.concatenate(
                    [grad[k * GROUP :], jnp.zeros((k * GROUP, BLOCK), F32)], axis=0
                )
            wide_ref[:total, k * BLOCK : (k + 1) * BLOCK] = early.astype(BF16)
        signal = group_rows(x_ref, g).astype(BF16)
        flipped = lax.dot_general(
            flip, signal, (((1,), (1,)), ((), ())), preferred_element_type=F32
        ).astype(BF16)
        high_ref[blocks] = jnp.zeros((8, BLOCK), F32)
        for d in range(0, blocks, LAGS):
            rows = total - d * GROUP
            weights = jnp.concatenate(
                [toeplitz_block(tile_ref, g, d + k) for k in range(LAGS)], axis=1
            )
            part = lax.dot_general(
                wide_ref[d * GROUP : total, :],
                weights,
                (((1,), (1,)), ((), ())),
                preferred_element_type=F32,
            )
            if d == 0:
                acc_ref[...] = part
            else:
                acc_ref[:rows, :] += part
            depth = total if 2 * d < blocks else total // 2
            cross_all = jnp.dot(
                flipped[:, :depth],
                wide_ref[d * GROUP : d * GROUP + depth, :],
                preferred_element_type=F32,
            )
            for k in range(LAGS):
                cross = cross_all[:, k * BLOCK : (k + 1) * BLOCK]
                s00, s01, s10, s11 = (turned(cross, r, l) for r in range(2) for l in range(2))
                low0 = jnp.where(wrapped, s01 + s10, s11)
                high0 = jnp.where(wrapped, zero, s00)
                low1 = jnp.where(wrapped, s11, zero)
                high1 = jnp.where(wrapped, s00, s01 + s10)
                low_ref[d + k] = jnp.concatenate([fold(low0), fold(low1)], axis=1)
                high_ref[d + k] = jnp.concatenate([fold(high0), fold(high1)], axis=1)
        parts.append(acc_ref[...].reshape(blocks, GROUP, BLOCK))
        rows = (low_ref[...] + high_ref[pl.ds(1, blocks)]).sum(axis=1) * scale
        for d in range(blocks):
            f_ref[g : g + 1, d * BLOCK : (d + 1) * BLOCK] = rows[d : d + 1]
    y_ref[...] = jnp.concatenate(parts, axis=1).astype(BF16)


def conv_forward(x, h):
    blocks = x.shape[0]
    total = blocks * GROUP
    return pl.pallas_call(
        conv_kernel,
        name="conv_forward",
        out_shape=jax.ShapeDtypeStruct(x.shape, BF16),
        scratch_shapes=[
            pltpu.VMEM((h.shape[0], h.shape[1] // HALF + 1, HALF, HALF), BF16),
            pltpu.VMEM((total, LAGS * BLOCK), BF16),
            pltpu.VMEM((total, BLOCK), F32),
        ],
        compiler_params=SCRATCH,
        cost_estimate=pl.CostEstimate(flops=6000000000, bytes_accessed=600000, transcendentals=0),
    )(x, h)


def conv_backward(m, x, h):
    blocks, chans, _ = x.shape
    total = blocks * GROUP
    scale = 1.0 / math.sqrt(GROUP * blocks * BLOCK)
    return pl.pallas_call(
        functools.partial(back_kernel, scale=scale),
        name="conv_backward",
        out_shape=(
            jax.ShapeDtypeStruct(x.shape, BF16),
            jax.ShapeDtypeStruct((chans // GROUP, blocks * BLOCK), F32),
        ),
        scratch_shapes=[
            pltpu.VMEM((h.shape[0], h.shape[1] // HALF + 1, HALF, HALF), BF16),
            pltpu.VMEM((total + total // 2, LAGS * BLOCK), BF16),
            pltpu.VMEM((total, BLOCK), F32),
            pltpu.VMEM((blocks, 8, BLOCK), F32),
            pltpu.VMEM((blocks + 1, 8, BLOCK), F32),
        ],
        compiler_params=SCRATCH,
        cost_estimate=pl.CostEstimate(flops=10000000000, bytes_accessed=1000000, transcendentals=0),
    )(m, x, h)


def met_places(at_ref, sign):
    z = at_ref[4]
    for first in (z, (z + 1) & 7, (z + 7) & 7, z ^ 2):
        for chan in (first, first ^ 4):
            yield (sign * ((chan & 3) - at_ref[3])) & 3, (chan >> 2) ^ at_ref[2]


def outside(array):
    return pltpu.with_memory_space_constraint(array, pltpu.HBM)


def piece_copy(source, target, sems, n):
    return pltpu.make_async_copy(source, target, sems.at[n])


def weight_copies(refs, buffer_ref, sems):
    return [piece_copy(ref, buffer_ref.at[n], sems, n) for n, ref in enumerate(refs)]


def all_columns(at_ref, pair, half, buffer_ref):
    first = at_ref[1] == 0
    own, own_c, side, side_c = (buffer_ref[pair * 4 + n, half] for n in range(4))
    parts = []
    for mine, other in ((own, own_c), (side, side_c)):
        parts += [jnp.where(first, mine, other), jnp.where(first, other, mine)]
    return jnp.concatenate(parts, axis=1)


def met_columns(at_ref, k, e, buffer_ref):
    z = at_ref[4]
    chan = ((at_ref[2] + e) & 1) * 4 + ((at_ref[3] + k) & 3)
    apart = (chan - z) & 3
    pair = jnp.where(apart == 0, 0, jnp.where(apart == 1, 1, jnp.where(apart == 3, 2, 3)))
    start = jnp.where(pair == 3, z ^ 2, (z + jnp.where(pair == 2, 7, pair)) & 7)
    return all_columns(at_ref, pair, jnp.where(chan == start, 0, 1), buffer_ref)


def side_columns(side, width):
    return pl.ds(pl.multiple_of(side * width, width), width)


def short_side(i, proj_ref, before_ref, taps_ref):
    now = proj_ref[i].astype(F32)
    before = before_ref[i].astype(F32)
    row = lax.broadcasted_iota(jnp.int32, now.shape, 0)
    total = taps_ref[i, SHORT - 1 : SHORT, :] * now
    for j in range(1, SHORT):
        late = pltpu.roll(now, j, 0)
        for r in range(j):
            late = jnp.where(row == r, before[SHORT - 1 - j + r][None, :], late)
        total = total + taps_ref[i, SHORT - 1 - j : SHORT - j, :] * late
    return total


def grad_mm_kernel(at_ref, proj_ref, before_ref, taps_ref, cot0, cot1, cot2, cot3, *refs):
    *w_refs, out_ref, mixed_ref, sent_ref, cots_ref, buffer_ref, cot_sems, sems = refs
    copies = weight_copies(w_refs, buffer_ref, sems)
    arrivals = [
        piece_copy(ref, cots_ref.at[n], cot_sems, n) for n, ref in enumerate((cot0, cot1, cot2, cot3))
    ]
    for copy in arrivals + copies:
        copy.start()
    query = short_side(0, proj_ref, before_ref, taps_ref)
    for copy in arrivals:
        copy.wait()
    yl = at_ref[0]
    width = cot0.shape[2] // 2
    for place, (k, e) in enumerate(met_places(at_ref, -1)):
        if place % 2 == 0:
            for copy in copies[place * 2 : place * 2 + 4]:
                copy.wait()
        lhs = jnp.concatenate(
            [cots_ref[k, e, :, side_columns(at, width)] for at in (yl, 1 - yl)], axis=1
        )
        part = lax.dot_general(
            lhs,
            all_columns(at_ref, place // 2, place % 2, buffer_ref),
            (((1,), (1,)), ((), ())),
            preferred_element_type=F32,
        )
        if place == 0:
            out_ref[...] = part
        else:
            out_ref[...] += part
    mixed = (out_ref[...] * query).astype(BF16)
    mixed_ref[...] = mixed
    sent_ref[...] = mixed.astype(F32).T.astype(BF16)


SCALARS = pl.BlockSpec(memory_space=pltpu.SMEM)
WHOLE = pl.BlockSpec(memory_space=pltpu.VMEM)
LEFT = pl.BlockSpec(memory_space=pl.ANY)


def grad_matmul(at, side_args, cots, ws):
    _, tok, rows = side_args[0].shape
    return pl.pallas_call(
        grad_mm_kernel,
        name="grad_matmul",
        out_shape=(
            OUTSIDE((tok, rows), F32),
            OUTSIDE((tok, rows), BF16),
            OUTSIDE((rows, tok), BF16),
        ),
        in_specs=[SCALARS] + [WHOLE] * len(side_args) + [LEFT] * (len(cots) + len(ws)),
        out_specs=(WHOLE,) * 3,
        scratch_shapes=[
            pltpu.VMEM((len(cots),) + cots[0].shape, BF16),
            pltpu.VMEM((len(ws),) + ws[0].shape, BF16),
            pltpu.SemaphoreType.DMA((len(cots),)),
            pltpu.SemaphoreType.DMA((len(ws),)),
        ],
        compiler_params=SCRATCH,
        cost_estimate=pl.CostEstimate(flops=4000000000, bytes_accessed=6500000, transcendentals=0),
    )(at, *side_args, *cots, *ws)


def mix_mm_kernel(at_ref, conv_ref, proj_ref, before_ref, taps_ref, skip_ref, grad_ref, *refs):
    *w_refs, out0, out1, out2, out3, query_grad_ref, parts_ref, buffer_ref, out_sems, sems = refs
    copies = weight_copies(w_refs, buffer_ref, sems)
    for copy in copies:
        copy.start()
    yl = at_ref[0]
    conv = conv_ref[...].astype(F32).T
    query, key, value = (short_side(i, proj_ref, before_ref, taps_ref) for i in range(3))
    mixed_in = conv + skip_ref[...] * (key * value).astype(BF16).astype(F32)
    query_grad_ref[...] = grad_ref[...] * mixed_in
    gated = (query * mixed_in).astype(BF16)
    width = parts_ref.shape[3] // 2
    for copy in copies:
        copy.wait()
    leaving = []
    for k, ref in enumerate((out0, out1, out2, out3)):
        for e in range(2):
            part = jnp.dot(
                gated, met_columns(at_ref, k, e, buffer_ref), preferred_element_type=F32
            ).astype(BF16)
            parts_ref[k, e, :, side_columns(yl, width)] = part[:, :width]
            parts_ref[k, e, :, side_columns(1 - yl, width)] = part[:, width:]
        leaving.append(piece_copy(parts_ref.at[k], ref, out_sems, k))
        leaving[-1].start()
    for copy in leaving:
        copy.wait()


def mix_matmul(at, conv, side_args, skip, grad, ws):
    tok, rows = grad.shape
    cols = 4 * ws[0].shape[-1]
    *parts, query_grad = pl.pallas_call(
        mix_mm_kernel,
        name="mix_matmul",
        out_shape=(OUTSIDE((2, tok, cols), BF16),) * 4 + (OUTSIDE((tok, rows), F32),),
        in_specs=[SCALARS] + [WHOLE] * (3 + len(side_args)) + [LEFT] * len(ws),
        out_specs=(LEFT,) * 4 + (WHOLE,),
        scratch_shapes=[
            pltpu.VMEM((4, 2, tok, cols), BF16),
            pltpu.VMEM((len(ws),) + ws[0].shape, BF16),
            pltpu.SemaphoreType.DMA((4,)),
            pltpu.SemaphoreType.DMA((len(ws),)),
        ],
        compiler_params=SCRATCH,
        cost_estimate=pl.CostEstimate(flops=4000000000, bytes_accessed=6500000, transcendentals=0),
    )(at, conv, *side_args, outside(skip), outside(grad), *ws)
    return parts, query_grad


def shift_z(shard, by):
    count = lax.axis_size("z")
    return lax.ppermute(shard, "z", [(i, (i + by) % count) for i in range(count)])


def cross_z(shard, by):
    return lax.ppermute(shard, "z", [(i, i ^ by) for i in range(lax.axis_size("z"))])


def shift_x(shard, by):
    count = lax.axis_size("x")
    return lax.ppermute(shard, "x", [(i, (i + by) % count) for i in range(count)])


def pre_kernel(proj_ref, before_ref, taps_ref, sent_ref):
    key, value = (short_side(i, proj_ref, before_ref, taps_ref) for i in (1, 2))
    sent_ref[...] = (key * value).T.astype(BF16)


def carried_columns(side_args):
    _, tok, cols = side_args[0].shape
    return pl.pallas_call(
        pre_kernel,
        name="carried_columns",
        out_shape=OUTSIDE((cols, tok), BF16),
        compiler_params=SCRATCH,
        cost_estimate=pl.CostEstimate(flops=5000000, bytes_accessed=1500000, transcendentals=0),
    )(*side_args)


def final_kernel(
    back_ref, mixed_ref, query_grad_ref, proj_ref, before_ref, taps_ref, skip_ref, out_ref, head_ref, tail_ref
):
    tok = mixed_ref.shape[0]
    row = lax.broadcasted_iota(jnp.int32, mixed_ref.shape, 0)
    carried_grad = back_ref[...].astype(F32).T + skip_ref[...] * mixed_ref[...].astype(F32)
    key, value = (short_side(i, proj_ref, before_ref, taps_ref) for i in (1, 2))
    grads = (query_grad_ref[...], carried_grad * value, carried_grad * key)
    for i, grad in enumerate(grads):
        head_ref[i] = grad[: head_ref.shape[1]]
        total = taps_ref[i, SHORT - 1 : SHORT, :] * grad
        for j in range(1, SHORT):
            early = jnp.where(row < tok - j, pltpu.roll(grad, tok - j, 0), 0.0)
            total = total + taps_ref[i, SHORT - 1 - j : SHORT - j, :] * early
        out_ref[i] = total.astype(BF16)
        tail_ref[i] = total[tok - EDGE :]


def final_short(back, mixed_grad, query_grad, side_args, skip):
    tok, cols = mixed_grad.shape
    return pl.pallas_call(
        final_kernel,
        name="final_short",
        out_shape=(
            jax.ShapeDtypeStruct((3, tok, cols), BF16),
            OUTSIDE((3, 8, cols), F32),
            jax.ShapeDtypeStruct((3, EDGE, cols), F32),
        ),
        compiler_params=SCRATCH,
        cost_estimate=pl.CostEstimate(flops=5000000, bytes_accessed=3500000, transcendentals=0),
    )(back, mixed_grad, query_grad, *side_args, outside(skip))


def edge_kernel(tail_ref, after_ref, taps_ref, whole_ref, out_ref):
    row = lax.broadcasted_iota(jnp.int32, tail_ref.shape[1:], 0)
    for i in range(3):
        after = after_ref[i]
        total = tail_ref[i]
        for s in range(SHORT - 1):
            missing = sum(
                taps_ref[i, SHORT - 2 - s - r : SHORT - 1 - s - r, :] * after[r : r + 1]
                for r in range(SHORT - 1 - s)
            )
            total = total + jnp.where(row == EDGE - 1 - s, 1.0, 0.0) * missing
        out_ref[i] = total.astype(BF16)


def edge_rows(tail, after, taps, whole):
    _, tok, cols = whole.shape
    return pl.pallas_call(
        edge_kernel,
        name="edge_rows",
        out_shape=jax.ShapeDtypeStruct(whole.shape, BF16),
        grid=(1,),
        in_specs=[
            pl.BlockSpec(tail.shape, lambda i: (0, 0, 0)),
            pl.BlockSpec(after.shape, lambda i: (0, 0, 0)),
            pl.BlockSpec(taps.shape, lambda i: (0, 0, 0)),
            pl.BlockSpec(memory_space=pl.ANY),
        ],
        out_specs=pl.BlockSpec((3, EDGE, cols), lambda i: (0, tok // EDGE - 1, 0)),
        input_output_aliases={3: 0},
        compiler_params=SCRATCH,
        cost_estimate=pl.CostEstimate(flops=500000, bytes_accessed=200000, transcendentals=0),
    )(tail, after, taps, whole)


def channel_major(sent):
    count = lax.axis_size(SEQ)
    sent = sent.reshape(count, sent.shape[0] // count, sent.shape[1])
    return lax.all_to_all(sent, SEQ, split_axis=0, concat_axis=0, tiled=True)


def token_major(block):
    got = lax.all_to_all(block, SEQ, split_axis=0, concat_axis=0, tiled=True)
    return got.reshape(got.shape[0] * got.shape[1], got.shape[2])


def on_device(projected, short_weight, filters, skip, out_weight, cotangent):
    tok_rows, _ = cotangent.shape
    rim = SHORT - 1
    wide, deep = lax.axis_size("x"), lax.axis_size("z")
    yl, core = lax.axis_index("yl"), lax.axis_index("core")
    yh, x, z = lax.axis_index("yh"), lax.axis_index("x"), lax.axis_index("z")

    at = jnp.stack([yl, core, yh, x, z]).astype(jnp.int32)
    before = from_behind(projected[tok_rows - rim :], 1)
    cot_pair = jnp.stack([cotangent, swap(cotangent, "yh")])
    cots = [cot_pair] + [shift_x(cot_pair, k) for k in range(1, wide)]
    w_pair = jnp.stack([out_weight, cross_z(out_weight, 4)])
    pairs = [shift_z(w_pair, deep - 1), shift_z(w_pair, 1), cross_z(w_pair, 2)]
    sides = [swap(w_pair, "yl")]
    sides += [swap(p, "yl") for p in pairs]
    pairs = [w_pair] + pairs
    pairs_c = [swap(p, "core") for p in pairs]
    sides_c = [swap(p, "core") for p in sides]
    ws = tuple(w for group in zip(pairs, pairs_c, sides, sides_c) for w in group)

    side_args = (projected.transpose(1, 0, 2), before.transpose(1, 0, 2), short_weight)
    carried_sent = carried_columns((outside(side_args[0]), side_args[1], outside(side_args[2])))
    carried_seq = channel_major(carried_sent)
    conv_seq = conv_forward(carried_seq, filters)
    conv = token_major(conv_seq)

    gated_grad, mixed_grad, grad_sent = grad_matmul(at, side_args, cots, ws)
    grad_seq = channel_major(grad_sent)

    parts, query_grad = mix_matmul(at, conv, side_args, skip[None, :], gated_grad, ws)
    shares = [parts[0]]
    for k in range(1, wide):
        shares.append(shift_x(parts[k], k))
    theirs = sum(p[1].astype(F32) for p in shares).astype(BF16)
    got = swap(theirs, "yh")
    mine = sum(p[0].astype(F32) for p in shares)
    mixed = (mine + got.astype(F32)).astype(BF16)

    back_seq, filter_grad = conv_backward(grad_seq, carried_seq, filters)
    back = token_major(back_seq)
    whole, head, tail = final_short(back, mixed_grad, query_grad, side_args, skip[None, :])
    after = from_behind(head, -1)
    projected_grad = edge_rows(tail, after, short_weight, whole)
    return (
        mixed,
        projected_grad.transpose(1, 0, 2),
        filter_grad,
    )


def solution(mesh):
    fine = Mesh(mesh.devices.reshape(8, 2, 2, 2, 4), ("z", "yl", "core", "yh", "x"))
    placed = (
        P(SEQ, None, CHAN),
        P(None, None, CHAN),
        P(CHAN + SEQ, None),
        P(CHAN),
        P(CHAN, SEQ),
        P(SEQ, CHAN),
    )
    return jax.shard_map(
        on_device,
        mesh=fine,
        in_specs=placed,
        out_specs=(P(SEQ, CHAN), P(SEQ, None, CHAN), P(CHAN + SEQ, None)),
        check_vma=False,
    )
```
